512 devices in a mesh: row: 8 (over z_lo, x), col: 8 (over z_hi, core), panel: 8 (over y).
Axes of the slice: x: 4, y: 8, z: 8 (z_hi: 4, z_lo: 2; z = z_hi * 2 + z_lo), core: 2. Of those that a mesh axis runs over, the one named last changes fastest.
Arguments:
- velocity: bfloat16 [4608, 6, 4096], P(('row', 'col'), None, 'panel'), may hold values from -6 to 6
- panel_weight: float32 [4096], P('panel'), may hold values from -0.109375 to 0.109375
- panel_group: int32 [4096], P('panel'), may hold values from 0 to 3
- tile_map: int32 [8, 8], replicated, may hold values from 0 to 3
- group_gain: float32 [4, 4], replicated, may hold values from 0.25 to 1
Outputs:
- qtf: float32 [4608, 2, 4608], P(('row', 'panel'), None, 'col')
The draws below stay inside these ranges and needn't reach their ends.
All inputs are finite; a program needn't handle non-finite values.
Results may differ from the reference program's by a relative error of at most 0.0029.
Values may be sent and summed in bfloat16 or wider, within the bound.
A program may use at most 64 MiB of HBM per device.

```python
import math
import jax
import jax.numpy as jnp
from jax import lax

GROUPS = 4
COLS = 4608
PANELS = 4096
N_ROW = 8
N_COL = 8


def with_ends(result, rng, smallest, high):
    dims = result.shape
    place = [jax.random.randint(jax.random.fold_in(rng, axis), (), 0, dims[axis]) for axis in range(len(dims))]
    result = result.at[tuple(place)].set(smallest)
    longest = dims.index(max(dims))
    place[longest] = (place[longest] + 1) % dims[longest]
    return result.at[tuple(place)].set(high)


def level_of(rng, shape, shards, smallest, largest):
    loudness, own = 1.0, jax.random.fold_in(rng, 6)
    for position, blocks in shards:
        heights = jnp.exp(jax.random.uniform(jax.random.fold_in(own, position), (blocks,), jnp.float32, smallest / len(shards), largest / len(shards)))
        loudness = loudness * jnp.repeat(heights, shape[position] // blocks).reshape([-1 if axis == position else 1 for axis in range(len(shape))])
    return loudness


def gaussian(stream_key, dims, spread, bound, cuts=(), dtype=jnp.bfloat16):
    result = spread * jax.random.normal(stream_key, dims, jnp.float32)
    if cuts:
        result = result * level_of(stream_key, dims, cuts, -0.22, 0.18)
    return jnp.clip(result, -bound, bound).astype(dtype)


def setup_inputs(seed: int = 0) -> dict:
    key_list = jax.random.split(jax.random.key(seed), 6)
    return {
        "velocity": gaussian(key_list[0], (COLS, 6, PANELS), 1.0, 6.0, ((0, 64), (2, 8))),
        "panel_weight": gaussian(key_list[1], (PANELS,), (3 * PANELS // 4) ** -0.5, 0.109375, ((0, 8),), jnp.float32),
        "panel_group": with_ends(jax.random.randint(key_list[2], (PANELS,), 0, GROUPS), jax.random.fold_in(key_list[2], 1), 0, GROUPS - 1).astype(jnp.int32),
        "tile_map": with_ends(jax.random.randint(key_list[3], (N_ROW, N_COL), 0, GROUPS), jax.random.fold_in(key_list[3], 1), 0, GROUPS - 1).astype(jnp.int32),
        "group_gain": jnp.clip(jnp.exp(jax.random.uniform(key_list[4], (GROUPS, GROUPS), jnp.float32, math.log(0.25), math.log(1.0))), 0.25, 1.0),
    }


def reference(velocity, panel_weight, panel_group, tile_map, group_gain):
    tile_width = COLS // N_ROW
    velocity_f32 = velocity.astype(jnp.float32)
    rows_out = []
    for row_tile in range(N_ROW):
        row_parts = []
        for col_tile in range(N_COL):
            region = tile_map[row_tile, col_tile]
            panel_scale = panel_weight * group_gain[panel_group, region]
            left_block = velocity_f32[row_tile * tile_width:(row_tile + 1) * tile_width]
            weighted = (left_block * panel_scale[None, None, :]).astype(jnp.bfloat16)
            weighted = lax.optimization_barrier(weighted).astype(jnp.float32)
            right_block = velocity_f32[col_tile * tile_width:(col_tile + 1) * tile_width]
            left_re = weighted[:, :3].reshape(tile_width, -1)
            left_im = weighted[:, 3:].reshape(tile_width, -1)
            right_re = right_block[:, :3].reshape(tile_width, -1)
            right_im = right_block[:, 3:].reshape(tile_width, -1)
            high = lax.Precision.HIGHEST
            gram_aa = jnp.dot(left_re, right_re.T, precision=high, preferred_element_type=jnp.float32)
            gram_ab = jnp.dot(left_re, right_im.T, precision=high, preferred_element_type=jnp.float32)
            gram_ba = jnp.dot(left_im, right_re.T, precision=high, preferred_element_type=jnp.float32)
            gram_bb = jnp.dot(left_im, right_im.T, precision=high, preferred_element_type=jnp.float32)
            tile_sign = 1.0 if row_tile <= col_tile else -1.0
            real_part = gram_aa + tile_sign * gram_bb
            imag_part = gram_ba - tile_sign * gram_ab
            row_parts.append(jnp.stack((real_part, imag_part), axis=1))
        rows_out.append(jnp.concatenate(row_parts, axis=2))
    return jnp.concatenate(rows_out, axis=0)
```

```python
import functools

import jax
import jax.numpy as jnp
from jax import lax
from jax.experimental import pallas as pl
from jax.experimental.pallas import tpu as pltpu
from jax.sharding import PartitionSpec as P

MESH = pl.DeviceIdType.MESH
NX = 4
NZ = 8
NY = 8


def device(x, z, core, y):
    return (lax.rem(z, 2) * NX + x, (z // 2) * 2 + core, y)


def kernel(
    v_ref, weight_ref, group_ref, case_ref, gain_ref, out_ref,
    rbuf, cbuf, scale, coef, acc, tbuf, ybuf, unit, piece, obuf,
    rsem, csem, ysem, osem, own_sem, near_sem, far_sem, cown_sem, cfwd_sem,
    part_sem, ysend_sem, osend_sem, local_sem,
):
    rows = v_ref.shape[1] // 2
    pair_rows = 4 * rows
    row, col, y = lax.axis_index("row"), lax.axis_index("col"), lax.axis_index("panel")
    zl, x = row // NX, lax.rem(row, NX)
    zh, core = col // 2, lax.rem(col, 2)
    z = 2 * zh + zl
    odd = lax.rem(zl + core, 2)
    tile_row = NX * core + x
    near = 2 - odd

    def chip_z(offset):
        return lax.rem(z + offset + NZ, NZ)

    def chip_x(offset):
        return lax.rem(x + offset + NX, NX)

    def final_owner(k):
        return (tile_row, NX * zl + k, y)

    is_final_self = jnp.logical_and(core == zl, col // NX == zl)
    final_self = lax.rem(col, NX)

    barrier = pltpu.get_barrier_semaphore()

    def greet(target):
        pl.semaphore_signal(barrier, inc=1, device_id=target, device_id_type=MESH)

    for dirn in (1, -1):
        for k in range(2):
            greet(device(x, chip_z(dirn), k, y))
        greet(device(chip_x(dirn), z, core, y))
    greet(device(x, z, 1 - core, y))
    for step in range(1, NY):
        greet((row, col, lax.rem(y + step, NY)))
    for h in range(NZ // 2):
        source_row = NX * (col // NX) + x
        source_col = 2 * h + zl
        @pl.when(jnp.logical_not(jnp.logical_and(is_final_self, h == zh)))
        def _():
            greet((source_row, source_col, y))
    pl.semaphore_wait(barrier, 18 - jnp.where(is_final_self, 1, 0))

    def remote(src, dst, send, recv, target):
        return pltpu.make_async_remote_copy(
            src_ref=src, dst_ref=dst, send_sem=send, recv_sem=recv,
            device_id=target, device_id_type=MESH,
        )

    def own_copy(target, c):
        where = (chip_z(1), chip_z(-1), z)[target]
        to = zl if target < 2 else 1 - core
        return remote(
            v_ref.at[c], rbuf.at[zh, c, core], own_sem.at[target, c],
            rsem.at[zh, c, core], device(x, where, to, y),
        )

    def cown_copy(target):
        to = device(chip_x(1 - 2 * target), z, core, y)
        return remote(v_ref, cbuf.at[x, :, core], cown_sem.at[target], csem.at[x, core], to)

    def part_copy(offset):
        src = v_ref if offset == 0 else cbuf.at[chip_x(offset), :, core]
        return remote(
            src, cbuf.at[chip_x(offset), :, core], part_sem.at[offset],
            csem.at[chip_x(offset), core], device(x, z, 1 - core, y),
        )

    local_c = pltpu.make_async_copy(v_ref, cbuf.at[x, :, core], local_sem.at[0])
    local_r = pltpu.make_async_copy(v_ref, rbuf.at[zh, :, core], local_sem.at[1])
    for c in range(3):
        own_copy(0, c).start()
        own_copy(1, c).start()
        if c == 0:
            cown_copy(0).start()
            cown_copy(1).start()
    part_copy(0).start()
    @pl.when(odd == 1)
    def _():
        for c in range(3):
            own_copy(2, c).start()
    local_c.start()
    @pl.when(odd == 0)
    def _():
        local_r.start()

    lanes = lax.broadcasted_iota(jnp.int32, (1, coef.shape[1]), 1)
    imag = lanes < 0
    for m in range(8):
        lo = m * 2 * rows + rows
        imag = jnp.logical_or(imag, jnp.logical_and(lanes >= lo, lanes < lo + rows))
    sign = jnp.zeros(lanes.shape, jnp.float32)
    for k in range(NX):
        tile_col = NX * zl + k
        case = case_ref[tile_row, tile_col]
        groups = group_ref[...]
        gain = jnp.zeros(groups.shape, jnp.float32)
        for g in range(gain_ref.shape[0]):
            gain = jnp.where(groups == g, gain_ref[g, case], gain)
        scale[pl.ds(k, 1), :] = weight_ref[...] * gain
        tile_sign = jnp.where(tile_row <= tile_col, 1.0, -1.0).astype(jnp.float32)
        sign = jnp.where(lanes >= pair_rows * k, tile_sign, sign)
    coef[pl.ds(0, 1), :] = jnp.where(imag, -sign, 1.0)
    coef[pl.ds(1, 1), :] = jnp.where(imag, 1.0, sign)

    def slot(offset):
        return chip_z(offset) // 2

    def arrival(h, c, k):
        return remote(
            rbuf.at[h, c, k], rbuf.at[h, c, k], own_sem.at[0, 0], rsem.at[h, c, k],
            device(x, chip_z(1), core, y),
        )

    def near_copy(side, c, k):
        dirn = 1 - 2 * side
        h = slot(-dirn * near)
        return remote(
            rbuf.at[h, c, k], rbuf.at[h, c, k], near_sem.at[side, c, k],
            rsem.at[h, c, k], device(x, chip_z(dirn), core, y),
        )

    def far_copy(side, c):
        dirn = 1 - 2 * side
        h = slot(-dirn * 3)
        return remote(
            rbuf.at[h, c, side], rbuf.at[h, c, side], far_sem.at[side, c],
            rsem.at[h, c, side], device(x, chip_z(dirn), core, y),
        )

    def near_step(c):
        for k in range(2):
            for side in range(2):
                arrival(slot((2 * side - 1) * near), c, k).wait_recv()
                near_copy(side, c, k).start()

    def far_step(c):
        for k in range(2):
            for side in range(2):
                arrival(slot((2 * side - 1) * 3), c, k).wait_recv()
                if k == side:
                    far_copy(side, c).start()

    def c_arrival(k, which):
        return remote(
            cbuf.at[k, :, which], cbuf.at[k, :, which], own_sem.at[0, 0],
            csem.at[k, which], device(x, z, 1 - core, y),
        )

    back = 2 * core - 1
    cfwd = remote(
        cbuf.at[chip_x(back), :, core], cbuf.at[chip_x(back), :, core], cfwd_sem.at[0],
        csem.at[chip_x(back), core], device(chip_x(-back), z, core, y),
    )

    @pl.when(odd == 1)
    def _():
        for c in range(3):
            near_step(c)
    c_arrival(chip_x(back), core).wait_recv()
    cfwd.start()
    c_arrival(chip_x(-back), core).wait_recv()
    part_copy(1).start()
    part_copy(3).start()
    @pl.when(odd == 0)
    def _():
        near_step(0)
    c_arrival(chip_x(2), core).wait_recv()
    part_copy(2).start()
    for offset in range(NX):
        c_arrival(chip_x(offset), 1 - core).wait_recv()
    local_c.wait()
    @pl.when(odd == 0)
    def _():
        local_r.wait()

    def pair_slot(pair):
        even_offset = 2 * (lax.rem(pair + pair // 2, 4) + 2 * (pair // 3))
        odd_offset = (2 * lax.rem(pair, 2) - 1) * (1 + 2 * (pair // 2))
        return slot(jnp.where(odd == 1, odd_offset, even_offset))

    def ysend(pair, k, p):
        return remote(
            tbuf.at[pair, k], ybuf.at[y], ysend_sem.at[pair, k], ysem.at[y], (row, col, p)
        )

    def finish(pair):
        h = pair_slot(pair)
        for k in range(2):
            base = k * 2 * rows
            top = jnp.concatenate([acc[j, base:base + rows, :] for j in range(NX)], axis=1)
            low = jnp.concatenate([acc[j, base + rows:base + 2 * rows, :] for j in range(NX)], axis=1)
            width = low.shape[1]
            swapped = jnp.where(
                imag, pltpu.roll(low, rows, 1), pltpu.roll(low, width - rows, 1)
            )
            total = coef[pl.ds(0, 1), :] * top + coef[pl.ds(1, 1), :] * swapped
            p = 2 * h + k
            @pl.when(p == y)
            def _():
                unit[...] = total
            @pl.when(p != y)
            def _():
                tbuf[pair, k] = total.astype(jnp.bfloat16)
                ysend(pair, k, p).start()

    def y_arrival(source):
        return remote(
            ybuf.at[source], ybuf.at[source], own_sem.at[0, 0], ysem.at[source],
            (row, col, lax.rem(y + 1, NY)),
        )

    def osend(k):
        return remote(
            piece.at[k], obuf.at[zh], osend_sem.at[k], osem.at[zh], final_owner(k)
        )

    def is_self(k):
        return jnp.logical_and(is_final_self, final_self == k)

    def reduce_unit():
        total = unit[...]
        for step in range(1, NY):
            source = lax.rem(y + step, NY)
            y_arrival(source).wait_recv()
            total = total + ybuf[source].astype(jnp.float32)
        for k in range(NX):
            part = total[:, k * pair_rows:(k + 1) * pair_rows]
            piece[k] = part
            @pl.when(is_self(k))
            def _():
                obuf[zh] = part
            @pl.when(jnp.logical_not(is_self(k)))
            def _():
                osend(k).start()

    my_h = y // 2

    def step_body(n, carry):
        pair, c = n // 3, lax.rem(n, 3)
        @pl.when(odd == 0)
        def _():
            @pl.when(pair == 0)
            def _():
                arrival(zh, c, 1 - core).wait_recv()
            @pl.when(jnp.logical_and(pair == 0, c > 0))
            def _():
                near_step(c)
            @pl.when(pair == 3)
            def _():
                for k in range(2):
                    arrival(slot(4), c, k).wait_recv()
        @pl.when(jnp.logical_and(odd == 1, pair == 2))
        def _():
            far_step(c)
        left = rbuf[pair_slot(pair), c].reshape(pair_rows, v_ref.shape[2]).astype(jnp.float32)
        for k in range(NX):
            weighted = (left * scale[pl.ds(k, 1), :]).astype(jnp.bfloat16)
            right = cbuf[k, c].reshape(pair_rows, v_ref.shape[2])
            product = lax.dot_general(
                weighted, right, (((1,), (1,)), ((), ())), preferred_element_type=jnp.float32
            )
            @pl.when(c == 0)
            def _():
                acc[k] = product
            @pl.when(c > 0)
            def _():
                acc[k] = acc[k] + product
        @pl.when(c == 2)
        def _():
            finish(pair)
            @pl.when(jnp.logical_or(
                jnp.logical_and(pair == 2, pair_slot(0) == my_h),
                jnp.logical_and(pair == 2, pair_slot(1) == my_h),
            ))
            def _():
                reduce_unit()
        return carry

    lax.fori_loop(0, 12, step_body, 0)
    @pl.when(jnp.logical_or(pair_slot(2) == my_h, pair_slot(3) == my_h))
    def _():
        reduce_unit()

    for h in range(NZ // 2):
        @pl.when(jnp.logical_not(jnp.logical_and(is_final_self, h == zh)))
        def _():
            remote(
                obuf.at[h], obuf.at[h], own_sem.at[0, 0], osem.at[h],
                device(x, z, 1 - core, y),
            ).wait_recv()
    got = [obuf[h] for h in range(NZ // 2)]
    for ri in range(2):
        out_ref[ri] = jnp.concatenate(
            [got[h][:, (2 * k + ri) * rows:(2 * k + ri + 1) * rows]
             for h in range(NZ // 2) for k in range(2)],
            axis=1,
        )

    for c in range(3):
        own_copy(0, c).wait_send()
        own_copy(1, c).wait_send()
        for side in range(2):
            for k in range(2):
                near_copy(side, c, k).wait_send()
    @pl.when(odd == 1)
    def _():
        for c in range(3):
            own_copy(2, c).wait_send()
            for side in range(2):
                far_copy(side, c).wait_send()
    cown_copy(0).wait_send()
    cown_copy(1).wait_send()
    cfwd.wait_send()
    for offset in range(NX):
        part_copy(offset).wait_send()
    for pair in range(4):
        for k in range(2):
            p = 2 * pair_slot(pair) + k
            @pl.when(p != y)
            def _():
                ysend(pair, k, p).wait_send()
    for k in range(NX):
        @pl.when(jnp.logical_not(is_self(k)))
        def _():
            osend(k).wait_send()


def local(velocity, panel_weight, panel_group, tile_map, group_gain):
    columns, parts, slab = velocity.shape
    half = parts // 2
    blocks = velocity.reshape(columns, 2, half, slab).transpose(2, 1, 0, 3)
    blocks = blocks.reshape(half, 2 * columns, slab)
    block = (half, 2, 2 * columns, slab)
    pair_rows = 4 * columns
    vmem = pl.BlockSpec(memory_space=pltpu.VMEM)
    smem = pl.BlockSpec(memory_space=pltpu.SMEM)
    dma = pltpu.SemaphoreType.DMA
    result = pl.pallas_call(
        kernel,
        out_shape=jax.ShapeDtypeStruct((2, columns, 8 * columns), jnp.float32),
        in_specs=[vmem, vmem, vmem, smem, smem],
        out_specs=vmem,
        scratch_shapes=[
            pltpu.VMEM((NZ // 2,) + block, jnp.bfloat16),
            pltpu.VMEM((NX,) + block, jnp.bfloat16),
            pltpu.VMEM((NX, slab), jnp.float32),
            pltpu.VMEM((2, NX * pair_rows), jnp.float32),
            pltpu.VMEM((NX, pair_rows, pair_rows), jnp.float32),
            pltpu.VMEM((4, 2, columns, NX * pair_rows), jnp.bfloat16),
            pltpu.VMEM((NY, columns, NX * pair_rows), jnp.bfloat16),
            pltpu.VMEM((columns, NX * pair_rows), jnp.float32),
            pltpu.VMEM((NX, columns, pair_rows), jnp.float32),
            pltpu.VMEM((NZ // 2, columns, pair_rows), jnp.float32),
            dma((NZ // 2, 3, 2)),
            dma((NX, 2)),
            dma((NY,)),
            dma((NZ // 2,)),
            dma((3, 3)),
            dma((2, 3, 2)),
            dma((2, 3)),
            dma((2,)),
            dma((1,)),
            dma((NX,)),
            dma((4, 2)),
            dma((NX,)),
            dma((2,)),
        ],
        compiler_params=pltpu.CompilerParams(
            collective_id=0, has_side_effects=True, vmem_limit_bytes=40 * 1024 * 1024
        ),
    )(blocks, panel_weight[None, :], panel_group[None, :], tile_map, group_gain)
    return result.transpose(1, 0, 2)


def solution(mesh):
    return jax.shard_map(
        local,
        mesh=mesh,
        in_specs=(P(("row", "col"), None, "panel"), P("panel"), P("panel"), P(), P()),
        out_specs=P(("row", "panel"), None, "col"),
        check_vma=False,
    )
```

```python
import functools

import jax
import jax.numpy as jnp
from jax import lax
from jax.experimental import pallas as pl
from jax.experimental.pallas import tpu as pltpu
from jax.sharding import PartitionSpec as P

MESH = pl.DeviceIdType.MESH
NX = 4
NZ = 8
NY = 8


def device(x, z, core, y):
    return (lax.rem(z, 2) * NX + x, (z // 2) * 2 + core, y)


def kernel(
    v_ref, weight_ref, group_ref, case_ref, gain_ref, out_ref,
    rbuf, cbuf, scale, coef, acc, own, tbuf, ybuf, piece, obuf,
    rsem, csem, ysem, osem, own_sem, near_sem, far_sem, cown_sem, cfwd_sem,
    part_sem, ysend_sem, osend_sem, local_sem,
):
    rows = v_ref.shape[1] // 2
    pair_rows = 4 * rows
    row, col, y = lax.axis_index("row"), lax.axis_index("col"), lax.axis_index("panel")
    zl, x = row // NX, lax.rem(row, NX)
    zh, core = col // 2, lax.rem(col, 2)
    z = 2 * zh + zl
    odd = lax.rem(zl + core, 2)
    tile_row = NX * core + x
    near = 2 - odd

    def chip_z(offset):
        return lax.rem(z + offset + NZ, NZ)

    def chip_x(offset):
        return lax.rem(x + offset + NX, NX)

    def final_owner(k):
        return (tile_row, NX * zl + k, y)

    is_final_self = jnp.logical_and(core == zl, col // NX == zl)
    final_self = lax.rem(col, NX)

    barrier = pltpu.get_barrier_semaphore()

    def greet(target):
        pl.semaphore_signal(barrier, inc=1, device_id=target, device_id_type=MESH)

    for dirn in (1, -1):
        for k in range(2):
            greet(device(x, chip_z(dirn), k, y))
        greet(device(chip_x(dirn), z, core, y))
    greet(device(x, z, 1 - core, y))
    for step in (1, NY - 1):
        greet((row, col, lax.rem(y + step, NY)))
    for h in range(NZ // 2):
        source_row = NX * (col // NX) + x
        source_col = 2 * h + zl
        @pl.when(jnp.logical_not(jnp.logical_and(is_final_self, h == zh)))
        def _():
            greet((source_row, source_col, y))
    pl.semaphore_wait(barrier, 13 - jnp.where(is_final_self, 1, 0))

    def remote(src, dst, send, recv, target):
        return pltpu.make_async_remote_copy(
            src_ref=src, dst_ref=dst, send_sem=send, recv_sem=recv,
            device_id=target, device_id_type=MESH,
        )

    def own_copy(target, c):
        where = (chip_z(1), chip_z(-1), z)[target]
        to = zl if target < 2 else 1 - core
        return remote(
            v_ref.at[c], rbuf.at[zh, c, core], own_sem.at[target, c],
            rsem.at[zh, c, core], device(x, where, to, y),
        )

    def cown_copy(target, c):
        to = device(chip_x(1 - 2 * target), z, core, y)
        return remote(
            v_ref.at[c], cbuf.at[x, c, core], cown_sem.at[target, c], csem.at[x, c, core], to
        )

    def part_copy(offset, c):
        k = chip_x(offset)
        src = v_ref.at[c] if offset == 0 else cbuf.at[k, c, core]
        return remote(
            src, cbuf.at[k, c, core], part_sem.at[offset, c], csem.at[k, c, core],
            device(x, z, 1 - core, y),
        )

    local_c = pltpu.make_async_copy(v_ref, cbuf.at[x, :, core], local_sem.at[0])
    local_r = pltpu.make_async_copy(v_ref, rbuf.at[zh, :, core], local_sem.at[1])
    for c in range(3):
        own_copy(0, c).start()
        own_copy(1, c).start()
        cown_copy(0, c).start()
        cown_copy(1, c).start()
        part_copy(0, c).start()
        @pl.when(odd == 1)
        def _():
            own_copy(2, c).start()
    local_c.start()
    @pl.when(odd == 0)
    def _():
        local_r.start()

    lanes = lax.broadcasted_iota(jnp.int32, (1, coef.shape[1]), 1)
    imag = lanes < 0
    for m in range(8):
        lo = m * 2 * rows + rows
        imag = jnp.logical_or(imag, jnp.logical_and(lanes >= lo, lanes < lo + rows))
    sign = jnp.zeros(lanes.shape, jnp.float32)
    for k in range(NX):
        tile_col = NX * zl + k
        case = case_ref[tile_row, tile_col]
        groups = group_ref[...]
        gain = jnp.zeros(groups.shape, jnp.float32)
        for g in range(gain_ref.shape[0]):
            gain = jnp.where(groups == g, gain_ref[g, case], gain)
        scale[pl.ds(k, 1), :] = weight_ref[...] * gain
        tile_sign = jnp.where(tile_row <= tile_col, 1.0, -1.0).astype(jnp.float32)
        sign = jnp.where(lanes >= pair_rows * k, tile_sign, sign)
    coef[pl.ds(0, 1), :] = jnp.where(imag, -sign, 1.0)
    coef[pl.ds(1, 1), :] = jnp.where(imag, 1.0, sign)

    def slot(offset):
        return chip_z(offset) // 2

    def arrival(h, c, k):
        return remote(
            rbuf.at[h, c, k], rbuf.at[h, c, k], own_sem.at[0, 0], rsem.at[h, c, k],
            device(x, chip_z(1), core, y),
        )

    def near_copy(side, c, k):
        dirn = 1 - 2 * side
        h = slot(-dirn * near)
        return remote(
            rbuf.at[h, c, k], rbuf.at[h, c, k], near_sem.at[side, c, k],
            rsem.at[h, c, k], device(x, chip_z(dirn), core, y),
        )

    def far_copy(side, c):
        dirn = 1 - 2 * side
        h = slot(-dirn * 3)
        return remote(
            rbuf.at[h, c, side], rbuf.at[h, c, side], far_sem.at[side, c],
            rsem.at[h, c, side], device(x, chip_z(dirn), core, y),
        )

    def near_step(c):
        for k in range(2):
            for side in range(2):
                arrival(slot((2 * side - 1) * near), c, k).wait_recv()
                near_copy(side, c, k).start()

    def far_step(c):
        for k in range(2):
            for side in range(2):
                arrival(slot((2 * side - 1) * 3), c, k).wait_recv()
                if k == side:
                    far_copy(side, c).start()

    def c_arrival(k, c, which):
        return remote(
            cbuf.at[k, c, which], cbuf.at[k, c, which], own_sem.at[0, 0],
            csem.at[k, c, which], device(x, z, 1 - core, y),
        )

    back = 2 * core - 1

    def cfwd_copy(c):
        k = chip_x(back)
        return remote(
            cbuf.at[k, c, core], cbuf.at[k, c, core], cfwd_sem.at[c],
            csem.at[k, c, core], device(chip_x(-back), z, core, y),
        )

    def c_step(c):
        c_arrival(chip_x(back), c, core).wait_recv()
        cfwd_copy(c).start()
        c_arrival(chip_x(-back), c, core).wait_recv()
        part_copy(1, c).start()
        part_copy(3, c).start()
        c_arrival(chip_x(2), c, core).wait_recv()
        part_copy(2, c).start()
        for offset in range(NX):
            c_arrival(chip_x(offset), c, 1 - core).wait_recv()

    local_c.wait()
    @pl.when(odd == 0)
    def _():
        local_r.wait()

    def pair_slot(pair):
        even_offset = 2 * (lax.rem(pair + pair // 2, 4) + 2 * (pair // 3))
        odd_offset = (2 * lax.rem(pair, 2) - 1) * (1 + 2 * (pair // 2))
        return slot(jnp.where(odd == 1, odd_offset, even_offset))

    third = own.shape[3]

    def role(pair, k):
        delta = lax.rem(y - (2 * pair_slot(pair) + k) + NY, NY)
        longest = NY // 2 - k
        down = delta <= longest
        stage = jnp.where(down, longest - delta, delta - (longest + 1))
        return delta, down, stage

    def ysend(pair, k, q):
        delta, down, _ = role(pair, k)
        unit = 2 * pair + k
        there = jnp.where(delta == NY - 1, NY, unit)
        to = lax.rem(y + jnp.where(down, NY - 1, 1), NY)
        return remote(
            tbuf.at[unit, q], ybuf.at[there, q], ysend_sem.at[unit, q], ysem.at[there, q],
            (row, col, to),
        )

    def y_arrival(unit, q):
        return remote(
            ybuf.at[unit, q], ybuf.at[unit, q], own_sem.at[0, 0], ysem.at[unit, q],
            (row, col, lax.rem(y + 1, NY)),
        )

    def finish(pair):
        for k in range(2):
            base = k * 2 * rows
            top = jnp.concatenate([acc[j, base:base + rows, :] for j in range(NX)], axis=1)
            low = jnp.concatenate([acc[j, base + rows:base + 2 * rows, :] for j in range(NX)], axis=1)
            width = low.shape[1]
            swapped = jnp.where(
                imag, pltpu.roll(low, rows, 1), pltpu.roll(low, width - rows, 1)
            )
            total = coef[pl.ds(0, 1), :] * top + coef[pl.ds(1, 1), :] * swapped
            delta, _, stage = role(pair, k)
            unit = 2 * pair + k
            is_head = jnp.logical_and(delta > 0, stage == 0)
            @pl.when(is_head)
            def _():
                for q in range(3):
                    tbuf[unit, q] = total[:, q * third:(q + 1) * third].astype(jnp.bfloat16)
                    ysend(pair, k, q).start()
            @pl.when(jnp.logical_not(is_head))
            def _():
                for q in range(3):
                    own[unit, q] = total[:, q * third:(q + 1) * third]

    def relay(pair, when):
        for k in range(2):
            delta, _, stage = role(pair, k)
            unit = 2 * pair + k
            @pl.when(jnp.logical_and(delta > 0, stage == when))
            def _():
                for q in range(3):
                    y_arrival(unit, q).wait_recv()
                    sums = own[unit, q] + ybuf[unit, q].astype(jnp.float32)
                    tbuf[unit, q] = sums.astype(jnp.bfloat16)
                    ysend(pair, k, q).start()

    def osend(k):
        return remote(
            piece.at[k], obuf.at[zh], osend_sem.at[k], osem.at[zh], final_owner(k)
        )

    def is_self(k):
        return jnp.logical_and(is_final_self, final_self == k)

    def reduce_unit(pair):
        unit = 2 * pair + lax.rem(y, 2)
        parts = []
        for q in range(3):
            y_arrival(unit, q).wait_recv()
            y_arrival(NY, q).wait_recv()
            parts.append(
                own[unit, q] + ybuf[unit, q].astype(jnp.float32) + ybuf[NY, q].astype(jnp.float32)
            )
        total = jnp.concatenate(parts, axis=1)
        for k in range(NX):
            part = total[:, k * pair_rows:(k + 1) * pair_rows]
            piece[k] = part
            @pl.when(is_self(k))
            def _():
                obuf[zh] = part
            @pl.when(jnp.logical_not(is_self(k)))
            def _():
                osend(k).start()

    def holds(pair):
        return pair_slot(pair) == y // 2

    def step_body(n, carry):
        pair, c = n // 3, lax.rem(n, 3)
        @pl.when(jnp.logical_or(jnp.logical_and(odd == 1, pair == 0), jnp.logical_and(odd == 0, n == 2)))
        def _():
            near_step(odd * n)
        @pl.when(pair == 0)
        def _():
            c_step(c)
        @pl.when(jnp.logical_and(odd == 0, jnp.logical_or(n == 2, n == 4)))
        def _():
            near_step(n // 2)
        @pl.when(jnp.logical_and(odd == 0, pair == 0))
        def _():
            arrival(zh, c, 1 - core).wait_recv()
        @pl.when(jnp.logical_and(odd == 0, pair == 3))
        def _():
            for k in range(2):
                arrival(slot(4), c, k).wait_recv()
        @pl.when(jnp.logical_and(odd == 1, pair == 2))
        def _():
            far_step(c)
        left = rbuf[pair_slot(pair), c].reshape(pair_rows, v_ref.shape[2]).astype(jnp.float32)
        for k in range(NX):
            weighted = (left * scale[pl.ds(k, 1), :]).astype(jnp.bfloat16)
            right = cbuf[k, c].reshape(pair_rows, v_ref.shape[2])
            product = lax.dot_general(
                weighted, right, (((1,), (1,)), ((), ())), preferred_element_type=jnp.float32
            )
            @pl.when(c == 0)
            def _():
                acc[k] = product
            @pl.when(c > 0)
            def _():
                acc[k] = acc[k] + product
        @pl.when(c == 2)
        def _():
            finish(pair)
        @pl.when(pair > 0)
        def _():
            relay(pair - 1, c + 1)
        @pl.when(jnp.logical_and(jnp.logical_and(pair > 1, c == 0), holds(pair - 2)))
        def _():
            reduce_unit(pair - 2)
        return carry

    lax.fori_loop(0, 12, step_body, 0)

    def tail_body(n, carry):
        relay(3, n + 1)
        @pl.when(jnp.logical_and(n == 0, holds(2)))
        def _():
            reduce_unit(2)
        return carry

    lax.fori_loop(0, 3, tail_body, 0)
    @pl.when(holds(3))
    def _():
        reduce_unit(3)

    for h in range(NZ // 2):
        @pl.when(jnp.logical_not(jnp.logical_and(is_final_self, h == zh)))
        def _():
            remote(
                obuf.at[h], obuf.at[h], own_sem.at[0, 0], osem.at[h],
                device(x, z, 1 - core, y),
            ).wait_recv()
    got = [obuf[h] for h in range(NZ // 2)]
    for ri in range(2):
        out_ref[ri] = jnp.concatenate(
            [got[h][:, (2 * k + ri) * rows:(2 * k + ri + 1) * rows]
             for h in range(NZ // 2) for k in range(2)],
            axis=1,
        )

    for c in range(3):
        own_copy(0, c).wait_send()
        own_copy(1, c).wait_send()
        for side in range(2):
            for k in range(2):
                near_copy(side, c, k).wait_send()
    @pl.when(odd == 1)
    def _():
        for c in range(3):
            own_copy(2, c).wait_send()
            for side in range(2):
                far_copy(side, c).wait_send()
    for c in range(3):
        cown_copy(0, c).wait_send()
        cown_copy(1, c).wait_send()
        cfwd_copy(c).wait_send()
        for offset in range(NX):
            part_copy(offset, c).wait_send()
    for pair in range(4):
        for k in range(2):
            @pl.when(role(pair, k)[0] > 0)
            def _():
                for q in range(3):
                    ysend(pair, k, q).wait_send()
    for k in range(NX):
        @pl.when(jnp.logical_not(is_self(k)))
        def _():
            osend(k).wait_send()


def local(velocity, panel_weight, panel_group, tile_map, group_gain):
    columns, parts, slab = velocity.shape
    half = parts // 2
    blocks = velocity.reshape(columns, 2, half, slab).transpose(2, 1, 0, 3)
    blocks = blocks.reshape(half, 2 * columns, slab)
    block = (half, 2, 2 * columns, slab)
    pair_rows = 4 * columns
    third = NX * pair_rows // 3
    vmem = pl.BlockSpec(memory_space=pltpu.VMEM)
    smem = pl.BlockSpec(memory_space=pltpu.SMEM)
    dma = pltpu.SemaphoreType.DMA
    result = pl.pallas_call(
        kernel,
        out_shape=jax.ShapeDtypeStruct((2, columns, 8 * columns), jnp.float32),
        in_specs=[vmem, vmem, vmem, smem, smem],
        out_specs=vmem,
        scratch_shapes=[
            pltpu.VMEM((NZ // 2,) + block, jnp.bfloat16),
            pltpu.VMEM((NX,) + block, jnp.bfloat16),
            pltpu.VMEM((NX, slab), jnp.float32),
            pltpu.VMEM((2, NX * pair_rows), jnp.float32),
            pltpu.VMEM((NX, pair_rows, pair_rows), jnp.float32),
            pltpu.VMEM((NY, 3, columns, third), jnp.float32),
            pltpu.VMEM((NY, 3, columns, third), jnp.bfloat16),
            pltpu.VMEM((NY + 1, 3, columns, third), jnp.bfloat16),
            pltpu.VMEM((NX, columns, pair_rows), jnp.float32),
            pltpu.VMEM((NZ // 2, columns, pair_rows), jnp.float32),
            dma((NZ // 2, 3, 2)),
            dma((NX, 3, 2)),
            dma((NY + 1, 3)),
            dma((NZ // 2,)),
            dma((3, 3)),
            dma((2, 3, 2)),
            dma((2, 3)),
            dma((2, 3)),
            dma((3,)),
            dma((NX, 3)),
            dma((NY, 3)),
            dma((NX,)),
            dma((2,)),
        ],
        compiler_params=pltpu.CompilerParams(
            collective_id=0, has_side_effects=True, vmem_limit_bytes=40 * 1024 * 1024
        ),
    )(blocks, panel_weight[None, :], panel_group[None, :], tile_map, group_gain)
    return result.transpose(1, 0, 2)


def solution(mesh):
    return jax.shard_map(
        local,
        mesh=mesh,
        in_specs=(P(("row", "col"), None, "panel"), P("panel"), P("panel"), P(), P()),
        out_specs=P(("row", "panel"), None, "col"),
        check_vma=False,
    )
```

```python
import functools

import jax
import jax.numpy as jnp
from jax import lax
from jax.experimental import pallas as pl
from jax.experimental.pallas import tpu as pltpu
from jax.sharding import PartitionSpec as P

MESH = pl.DeviceIdType.MESH
NX = 4
NZ = 8
NY = 8


def device(x, z, core, y):
    return (lax.rem(z, 2) * NX + x, (z // 2) * 2 + core, y)


def kernel(
    v_ref, weight_ref, group_ref, case_ref, gain_ref, out_ref,
    rbuf, cbuf, scale, acc, own, tbuf, ybuf, piece, obuf,
    rsem, csem, ysem, osem, own_sem, near_sem, far_sem, cown_sem, cfwd_sem,
    part_sem, ysend_sem, osend_sem, local_sem,
):
    rows = v_ref.shape[1] // 2
    pair_rows = 4 * rows
    row, col, y = lax.axis_index("row"), lax.axis_index("col"), lax.axis_index("panel")
    zl, x = row // NX, lax.rem(row, NX)
    zh, core = col // 2, lax.rem(col, 2)
    z = 2 * zh + zl
    odd = lax.rem(zl + core, 2)
    tile_row = NX * core + x
    near = 2 - odd

    def chip_z(offset):
        return lax.rem(z + offset + NZ, NZ)

    def chip_x(offset):
        return lax.rem(x + offset + NX, NX)

    def chip_y(offset):
        return lax.rem(y + offset + NY, NY)

    is_final_self = jnp.logical_and(
        jnp.logical_and(core == zl, col == NX * zl + lax.rem(y, NX)), y // NX == lax.rem(y, 2)
    )

    barrier = pltpu.get_barrier_semaphore()

    def greet(target):
        pl.semaphore_signal(barrier, inc=1, device_id=target, device_id_type=MESH)

    for dirn in (1, -1):
        for k in range(2):
            greet(device(x, chip_z(dirn), k, y))
        greet(device(chip_x(dirn), z, core, y))
    greet(device(x, z, 1 - core, y))
    for offset in (1, -1, 2, -2):
        greet((row, col, chip_y(offset)))
    for h in range(NZ // 2):
        source_row = NX * (col // NX) + x
        source_col = 2 * h + zl
        @pl.when(jnp.logical_not(jnp.logical_and(is_final_self, h == zh)))
        def _():
            greet((source_row, source_col, NX * lax.rem(y, 2) + lax.rem(col, NX)))
    pl.semaphore_wait(barrier, 15 - jnp.where(is_final_self, 1, 0))

    def remote(src, dst, send, recv, target):
        return pltpu.make_async_remote_copy(
            src_ref=src, dst_ref=dst, send_sem=send, recv_sem=recv,
            device_id=target, device_id_type=MESH,
        )

    def own_copy(target, c):
        where = (chip_z(1), chip_z(-1), z)[target]
        to = zl if target < 2 else 1 - core
        return remote(
            v_ref.at[c], rbuf.at[zh, c, core], own_sem.at[target, c],
            rsem.at[zh, c, core], device(x, where, to, y),
        )

    def cown_copy(target, c):
        to = device(chip_x(1 - 2 * target), z, core, y)
        return remote(
            v_ref.at[c], cbuf.at[x, c, core], cown_sem.at[target, c], csem.at[x, c, core], to
        )

    def part_copy(offset, c):
        k = chip_x(offset)
        src = v_ref.at[c] if offset == 0 else cbuf.at[k, c, core]
        return remote(
            src, cbuf.at[k, c, core], part_sem.at[offset, c], csem.at[k, c, core],
            device(x, z, 1 - core, y),
        )

    local_c = pltpu.make_async_copy(v_ref, cbuf.at[x, :, core], local_sem.at[0])
    local_r = pltpu.make_async_copy(v_ref, rbuf.at[zh, :, core], local_sem.at[1])
    for c in range(3):
        own_copy(0, c).start()
        own_copy(1, c).start()
        if c == 0:
            cown_copy(0, c).start()
            cown_copy(1, c).start()
        part_copy(0, c).start()
        @pl.when(odd == 1)
        def _():
            own_copy(2, c).start()
    local_c.start()
    @pl.when(odd == 0)
    def _():
        local_r.start()

    lanes = lax.broadcasted_iota(jnp.int32, (1, acc.shape[2]), 1)
    imag = jnp.logical_or(
        jnp.logical_and(lanes >= rows, lanes < 2 * rows),
        jnp.logical_and(lanes >= 3 * rows, lanes < 4 * rows),
    )
    for k in range(NX):
        case = case_ref[tile_row, NX * zl + k]
        groups = group_ref[...]
        gain = jnp.zeros(groups.shape, jnp.float32)
        for g in range(gain_ref.shape[0]):
            gain = jnp.where(groups == g, gain_ref[g, case], gain)
        scale[pl.ds(k, 1), :] = weight_ref[...] * gain

    def slot(offset):
        return chip_z(offset) // 2

    def arrival(h, c, k):
        return remote(
            rbuf.at[h, c, k], rbuf.at[h, c, k], own_sem.at[0, 0], rsem.at[h, c, k],
            device(x, chip_z(1), core, y),
        )

    def near_copy(side, c, k):
        dirn = 1 - 2 * side
        h = slot(-dirn * near)
        return remote(
            rbuf.at[h, c, k], rbuf.at[h, c, k], near_sem.at[side, c, k],
            rsem.at[h, c, k], device(x, chip_z(dirn), core, y),
        )

    def far_copy(side, c):
        dirn = 1 - 2 * side
        h = slot(-dirn * 3)
        return remote(
            rbuf.at[h, c, side], rbuf.at[h, c, side], far_sem.at[side, c],
            rsem.at[h, c, side], device(x, chip_z(dirn), core, y),
        )

    def near_step(c):
        for k in range(2):
            for side in range(2):
                arrival(slot((2 * side - 1) * near), c, k).wait_recv()
                near_copy(side, c, k).start()

    def far_step(c):
        for k in range(2):
            for side in range(2):
                arrival(slot((2 * side - 1) * 3), c, k).wait_recv()
                if k == side:
                    far_copy(side, c).start()

    def c_arrival(k, c, which):
        return remote(
            cbuf.at[k, c, which], cbuf.at[k, c, which], own_sem.at[0, 0],
            csem.at[k, c, which], device(x, z, 1 - core, y),
        )

    back = 2 * core - 1

    def cfwd_copy(c):
        k = chip_x(back)
        return remote(
            cbuf.at[k, c, core], cbuf.at[k, c, core], cfwd_sem.at[c],
            csem.at[k, c, core], device(chip_x(-back), z, core, y),
        )

    def c_step(c):
        c_arrival(chip_x(back), c, core).wait_recv()
        cfwd_copy(c).start()
        @pl.when(c < 2)
        def _():
            cown_copy(0, c + 1).start()
            cown_copy(1, c + 1).start()
        c_arrival(chip_x(-back), c, core).wait_recv()
        part_copy(1, c).start()
        part_copy(3, c).start()
        c_arrival(chip_x(2), c, core).wait_recv()
        part_copy(2, c).start()
        for offset in range(NX):
            c_arrival(chip_x(offset), c, 1 - core).wait_recv()

    local_c.wait()
    @pl.when(odd == 0)
    def _():
        local_r.wait()

    def pair_slot(pair):
        even_offset = 2 * (lax.rem(pair + pair // 2, 4) + 2 * (pair // 3))
        odd_offset = (2 * lax.rem(pair, 2) - 1) * (1 + 2 * (pair // 2))
        return slot(jnp.where(odd == 1, odd_offset, even_offset))

    def ysend(pair, i):
        flip = lax.rem(y, 2)
        hop = (-1, 1, -1, 1, -2 + 4 * flip, -2, 2)[i]
        there = (0, 1, 4, 6, 5, 2, 3)[i]
        return remote(
            tbuf.at[pair, i], ybuf.at[pair, there], ysend_sem.at[pair, i],
            ysem.at[pair, there], (row, col, chip_y(hop)),
        )

    def y_arrival(pair, i):
        return remote(
            ybuf.at[pair, i], ybuf.at[pair, i], own_sem.at[0, 0], ysem.at[pair, i],
            (row, col, chip_y(1)),
        )

    def y_value(pair, i):
        y_arrival(pair, i).wait_recv()
        return ybuf[pair, i].astype(jnp.float32)

    def finish(pair):
        width = 4 * rows
        for j in range(NX):
            sign = jnp.where(tile_row <= NX * zl + j, 1.0, -1.0).astype(jnp.float32)
            for k in range(2):
                base = k * 2 * rows
                top = acc[j, base:base + rows, :]
                low = acc[j, base + rows:base + 2 * rows, :]
                swapped = jnp.where(
                    imag, pltpu.roll(low, rows, 1), pltpu.roll(low, acc.shape[2] - rows, 1)
                )
                total = jnp.where(imag, swapped - sign * top, top + sign * swapped)
                own[pair, NX * k + j] = total[:, :width]
        for i, delta in enumerate((1, -1, 3, -3, 4)):
            tbuf[pair, i] = own[pair, chip_y(-delta)].astype(jnp.bfloat16)
            ysend(pair, i).start()

    def relay(pair):
        for side in range(2):
            total = own[pair, chip_y(-2 + 4 * side)] + y_value(pair, 4 + 2 * side)
            @pl.when(lax.rem(y, 2) == side)
            def _():
                tbuf[pair, 5 + side] = (total + y_value(pair, 5)).astype(jnp.bfloat16)
            @pl.when(lax.rem(y, 2) != side)
            def _():
                tbuf[pair, 5 + side] = total.astype(jnp.bfloat16)
            ysend(pair, 5 + side).start()

    def osend(pair):
        p = 2 * pair_slot(pair) + y // NX
        target = (tile_row, NX * zl + lax.rem(y, NX), p)
        return remote(
            piece.at[pair], obuf.at[zh], osend_sem.at[pair], osem.at[zh], target
        )

    def is_self(pair):
        return jnp.logical_and(is_final_self, pair_slot(pair) == y // 2)

    def reduce_unit(pair):
        total = own[pair, y]
        for i in range(4):
            total = total + y_value(pair, i)
        @pl.when(is_self(pair))
        def _():
            obuf[zh] = total
        @pl.when(jnp.logical_not(is_self(pair)))
        def _():
            piece[pair] = total
            osend(pair).start()

    def step_body(n, carry):
        pair, c = n // 3, lax.rem(n, 3)
        @pl.when(jnp.logical_or(jnp.logical_and(odd == 1, pair == 0), jnp.logical_and(odd == 0, n == 2)))
        def _():
            near_step(odd * n)
        @pl.when(pair == 0)
        def _():
            c_step(c)
        @pl.when(jnp.logical_and(odd == 0, jnp.logical_or(n == 2, n == 4)))
        def _():
            near_step(n // 2)
        @pl.when(jnp.logical_and(odd == 0, pair == 0))
        def _():
            arrival(zh, c, 1 - core).wait_recv()
        @pl.when(jnp.logical_and(odd == 0, pair == 3))
        def _():
            for k in range(2):
                arrival(slot(4), c, k).wait_recv()
        @pl.when(jnp.logical_and(odd == 1, pair == 2))
        def _():
            far_step(c)
        left = rbuf[pair_slot(pair), c].reshape(pair_rows, v_ref.shape[2]).astype(jnp.float32)
        for k in range(NX):
            weighted = (left * scale[pl.ds(k, 1), :]).astype(jnp.bfloat16)
            right = cbuf[k, c].reshape(pair_rows, v_ref.shape[2])
            product = lax.dot_general(
                weighted, right, (((1,), (1,)), ((), ())), preferred_element_type=jnp.float32
            )
            @pl.when(c == 0)
            def _():
                acc[k, :, :pair_rows] = product
            @pl.when(c > 0)
            def _():
                acc[k, :, :pair_rows] = acc[k, :, :pair_rows] + product
        @pl.when(c == 2)
        def _():
            finish(pair)
        @pl.when(jnp.logical_and(pair > 0, c == 1))
        def _():
            relay(pair - 1)
        @pl.when(jnp.logical_and(pair > 1, c == 0))
        def _():
            reduce_unit(pair - 2)
        return carry

    for k in range(NX):
        acc[k, :, pair_rows:] = jnp.zeros((pair_rows, acc.shape[2] - pair_rows), jnp.float32)
    lax.fori_loop(0, 12, step_body, 0)
    reduce_unit(2)
    relay(3)
    reduce_unit(3)

    for h in range(NZ // 2):
        @pl.when(jnp.logical_not(jnp.logical_and(is_final_self, h == zh)))
        def _():
            remote(
                obuf.at[h], obuf.at[h], own_sem.at[0, 0], osem.at[h],
                device(x, z, 1 - core, y),
            ).wait_recv()
    got = [obuf[h] for h in range(NZ // 2)]
    for ri in range(2):
        out_ref[ri] = jnp.concatenate(
            [got[h][:, (2 * k + ri) * rows:(2 * k + ri + 1) * rows]
             for h in range(NZ // 2) for k in range(2)],
            axis=1,
        )

    for c in range(3):
        own_copy(0, c).wait_send()
        own_copy(1, c).wait_send()
        for side in range(2):
            for k in range(2):
                near_copy(side, c, k).wait_send()
    @pl.when(odd == 1)
    def _():
        for c in range(3):
            own_copy(2, c).wait_send()
            for side in range(2):
                far_copy(side, c).wait_send()
    for c in range(3):
        cown_copy(0, c).wait_send()
        cown_copy(1, c).wait_send()
        cfwd_copy(c).wait_send()
        for offset in range(NX):
            part_copy(offset, c).wait_send()
    for pair in range(4):
        for i in range(7):
            ysend(pair, i).wait_send()
        @pl.when(jnp.logical_not(is_self(pair)))
        def _():
            osend(pair).wait_send()


def local(velocity, panel_weight, panel_group, tile_map, group_gain):
    columns, parts, slab = velocity.shape
    half = parts // 2
    blocks = velocity.reshape(columns, 2, half, slab).transpose(2, 1, 0, 3)
    blocks = blocks.reshape(half, 2 * columns, slab)
    block = (half, 2, 2 * columns, slab)
    pair_rows = 4 * columns
    vmem = pl.BlockSpec(memory_space=pltpu.VMEM)
    smem = pl.BlockSpec(memory_space=pltpu.SMEM)
    dma = pltpu.SemaphoreType.DMA
    result = pl.pallas_call(
        kernel,
        out_shape=jax.ShapeDtypeStruct((2, columns, 8 * columns), jnp.float32),
        in_specs=[vmem, vmem, vmem, smem, smem],
        out_specs=vmem,
        scratch_shapes=[
            pltpu.VMEM((NZ // 2,) + block, jnp.bfloat16),
            pltpu.VMEM((NX,) + block, jnp.bfloat16),
            pltpu.VMEM((NX, slab), jnp.float32),
            pltpu.VMEM((NX, pair_rows, pl.cdiv(pair_rows, 128) * 128), jnp.float32),
            pltpu.VMEM((4, NY, columns, pair_rows), jnp.float32),
            pltpu.VMEM((4, 7, columns, pair_rows), jnp.bfloat16),
            pltpu.VMEM((4, 7, columns, pair_rows), jnp.bfloat16),
            pltpu.VMEM((NX, columns, pair_rows), jnp.float32),
            pltpu.VMEM((NZ // 2, columns, pair_rows), jnp.float32),
            dma((NZ // 2, 3, 2)),
            dma((NX, 3, 2)),
            dma((4, 7)),
            dma((NZ // 2,)),
            dma((3, 3)),
            dma((2, 3, 2)),
            dma((2, 3)),
            dma((2, 3)),
            dma((3,)),
            dma((NX, 3)),
            dma((4, 7)),
            dma((NX,)),
            dma((2,)),
        ],
        compiler_params=pltpu.CompilerParams(
            collective_id=0, has_side_effects=True, vmem_limit_bytes=40 * 1024 * 1024
        ),
    )(blocks, panel_weight[None, :], panel_group[None, :], tile_map, group_gain)
    return result.transpose(1, 0, 2)


def solution(mesh):
    return jax.shard_map(
        local,
        mesh=mesh,
        in_specs=(P(("row", "col"), None, "panel"), P("panel"), P("panel"), P(), P()),
        out_specs=P(("row", "panel"), None, "col"),
        check_vma=False,
    )
```

```python
import functools

import jax
import jax.numpy as jnp
from jax import lax
from jax.experimental import pallas as pl
from jax.experimental.pallas import tpu as pltpu
from jax.sharding import PartitionSpec as P

MESH = pl.DeviceIdType.MESH
NX = 4
NZ = 8
NY = 8


def device(x, z, core, y):
    return (lax.rem(z, 2) * NX + x, (z // 2) * 2 + core, y)


def kernel(
    v_ref, weight_ref, group_ref, case_ref, gain_ref, out_ref,
    rbuf, cbuf, scale, acc, own, tbuf, ybuf, piece, obuf,
    rsem, csem, ysem, osem, own_sem, near_sem, far_sem, cown_sem, cfwd_sem,
    part_sem, ysend_sem, osend_sem, local_sem,
):
    rows = v_ref.shape[1] // 2
    pair_rows = 4 * rows
    row, col, y = lax.axis_index("row"), lax.axis_index("col"), lax.axis_index("panel")
    zl, x = row // NX, lax.rem(row, NX)
    zh, core = col // 2, lax.rem(col, 2)
    z = 2 * zh + zl
    odd = lax.rem(zl + core, 2)
    tile_row = NX * core + x
    near = 2 - odd

    def chip_z(offset):
        return lax.rem(z + offset + NZ, NZ)

    def chip_x(offset):
        return lax.rem(x + offset + NX, NX)

    def chip_y(offset):
        return lax.rem(y + offset + NY, NY)

    mine = lax.rem(y, NX)
    is_final_self = jnp.logical_and(core == zl, col == NX * zl + mine)

    def is_local(h, g):
        return jnp.logical_and(is_final_self, jnp.logical_and(h == zh, g == y // NX))

    barrier = pltpu.get_barrier_semaphore()

    def greet(target):
        pl.semaphore_signal(barrier, inc=1, device_id=target, device_id_type=MESH)

    for dirn in (1, -1):
        for k in range(2):
            greet(device(x, chip_z(dirn), k, y))
        greet(device(chip_x(dirn), z, core, y))
    greet(device(x, z, 1 - core, y))
    for offset in (1, -1, 2, -2):
        greet((row, col, chip_y(offset)))
    for h in range(NZ // 2):
        for g in range(2):
            source = (NX * (col // NX) + x, 2 * h + zl, NX * g + lax.rem(col, NX))
            @pl.when(jnp.logical_not(is_local(h, g)))
            def _():
                greet(source)
    pl.semaphore_wait(barrier, 19 - jnp.where(is_final_self, 1, 0))

    def remote(src, dst, send, recv, target):
        return pltpu.make_async_remote_copy(
            src_ref=src, dst_ref=dst, send_sem=send, recv_sem=recv,
            device_id=target, device_id_type=MESH,
        )

    def own_copy(target, c):
        where = (chip_z(1), chip_z(-1), z)[target]
        to = zl if target < 2 else 1 - core
        return remote(
            v_ref.at[c], rbuf.at[zh, c, core], own_sem.at[target, c],
            rsem.at[zh, c, core], device(x, where, to, y),
        )

    def cown_copy(target, c):
        to = device(chip_x(1 - 2 * target), z, core, y)
        return remote(
            v_ref.at[c], cbuf.at[x, c, core], cown_sem.at[target, c], csem.at[x, c, core], to
        )

    def part_copy(offset, c):
        k = chip_x(offset)
        src = v_ref.at[c] if offset == 0 else cbuf.at[k, c, core]
        return remote(
            src, cbuf.at[k, c, core], part_sem.at[offset, c], csem.at[k, c, core],
            device(x, z, 1 - core, y),
        )

    local_c = pltpu.make_async_copy(v_ref, cbuf.at[x, :, core], local_sem.at[0])
    local_r = pltpu.make_async_copy(v_ref, rbuf.at[zh, :, core], local_sem.at[1])
    for c in range(3):
        own_copy(0, c).start()
        own_copy(1, c).start()
        if c == 0:
            cown_copy(0, c).start()
            cown_copy(1, c).start()
        part_copy(0, c).start()
        @pl.when(odd == 1)
        def _():
            own_copy(2, c).start()
    local_c.start()
    @pl.when(odd == 0)
    def _():
        local_r.start()

    lanes = lax.broadcasted_iota(jnp.int32, (1, acc.shape[2]), 1)
    imag = jnp.logical_or(
        jnp.logical_and(lanes >= rows, lanes < 2 * rows),
        jnp.logical_and(lanes >= 3 * rows, lanes < 4 * rows),
    )
    for k in range(NX):
        case = case_ref[tile_row, NX * zl + k]
        groups = group_ref[...]
        gain = jnp.zeros(groups.shape, jnp.float32)
        for g in range(gain_ref.shape[0]):
            gain = jnp.where(groups == g, gain_ref[g, case], gain)
        scale[pl.ds(k, 1), :] = weight_ref[...] * gain

    def slot(offset):
        return chip_z(offset) // 2

    def arrival(h, c, k):
        return remote(
            rbuf.at[h, c, k], rbuf.at[h, c, k], own_sem.at[0, 0], rsem.at[h, c, k],
            device(x, chip_z(1), core, y),
        )

    def near_copy(side, c, k):
        dirn = 1 - 2 * side
        h = slot(-dirn * near)
        return remote(
            rbuf.at[h, c, k], rbuf.at[h, c, k], near_sem.at[side, c, k],
            rsem.at[h, c, k], device(x, chip_z(dirn), core, y),
        )

    def far_copy(side, c):
        dirn = 1 - 2 * side
        h = slot(-dirn * 3)
        return remote(
            rbuf.at[h, c, side], rbuf.at[h, c, side], far_sem.at[side, c],
            rsem.at[h, c, side], device(x, chip_z(dirn), core, y),
        )

    def near_step(c):
        for k in range(2):
            for side in range(2):
                arrival(slot((2 * side - 1) * near), c, k).wait_recv()
                near_copy(side, c, k).start()

    def far_step(c):
        for k in range(2):
            for side in range(2):
                arrival(slot((2 * side - 1) * 3), c, k).wait_recv()
                if k == side:
                    far_copy(side, c).start()

    def c_arrival(k, c, which):
        return remote(
            cbuf.at[k, c, which], cbuf.at[k, c, which], own_sem.at[0, 0],
            csem.at[k, c, which], device(x, z, 1 - core, y),
        )

    back = 2 * core - 1

    def cfwd_copy(c):
        k = chip_x(back)
        return remote(
            cbuf.at[k, c, core], cbuf.at[k, c, core], cfwd_sem.at[c],
            csem.at[k, c, core], device(chip_x(-back), z, core, y),
        )

    def c_step(c):
        c_arrival(chip_x(back), c, core).wait_recv()
        cfwd_copy(c).start()
        @pl.when(c < 2)
        def _():
            cown_copy(0, c + 1).start()
            cown_copy(1, c + 1).start()
        c_arrival(chip_x(-back), c, core).wait_recv()
        part_copy(1, c).start()
        part_copy(3, c).start()
        c_arrival(chip_x(2), c, core).wait_recv()
        part_copy(2, c).start()
        for offset in range(NX):
            c_arrival(chip_x(offset), c, 1 - core).wait_recv()

    local_c.wait()
    @pl.when(odd == 0)
    def _():
        local_r.wait()

    def pair_slot(pair):
        even_offset = 2 * (lax.rem(pair + pair // 2, 4) + 2 * (pair // 3))
        odd_offset = (2 * lax.rem(pair, 2) - 1) * (1 + 2 * (pair // 2))
        return slot(jnp.where(odd == 1, odd_offset, even_offset))

    def ysend(pair, i):
        hop = (1, -1, 4 * lax.rem(y, 2) - 2)[i]
        return remote(
            tbuf.at[pair, lax.rem(chip_y(hop), NX)], ybuf.at[pair, i], ysend_sem.at[pair, i],
            ysem.at[pair, i], (row, col, chip_y(hop)),
        )

    def y_arrival(pair, i):
        return remote(
            ybuf.at[pair, i], ybuf.at[pair, i], own_sem.at[0, 0], ysem.at[pair, i],
            (row, col, chip_y(1)),
        )

    def finish(pair):
        for j in range(NX):
            sign = jnp.where(tile_row <= NX * zl + j, 1.0, -1.0).astype(jnp.float32)
            halves = []
            for k in range(2):
                base = k * 2 * rows
                top = acc[j, base:base + rows, :]
                low = acc[j, base + rows:base + 2 * rows, :]
                swapped = jnp.where(
                    imag, pltpu.roll(low, rows, 1), pltpu.roll(low, acc.shape[2] - rows, 1)
                )
                halves.append(jnp.where(imag, swapped - sign * top, top + sign * swapped))
            total = jnp.concatenate(halves, axis=0)[:, :pair_rows]
            @pl.when(mine == j)
            def _():
                own[pair] = total
            @pl.when(mine != j)
            def _():
                tbuf[pair, j] = total.astype(jnp.bfloat16)
        for i in range(3):
            ysend(pair, i).start()

    def osend(pair, k):
        target = (tile_row, NX * zl + mine, 2 * pair_slot(pair) + k)
        there = y // NX
        return remote(
            piece.at[pair, k], obuf.at[zh, there], osend_sem.at[pair, k], osem.at[zh, there], target
        )

    def is_self(pair, k):
        return jnp.logical_and(is_final_self, 2 * pair_slot(pair) + k == y)

    def relay(pair):
        total = own[pair]
        for i in range(3):
            y_arrival(pair, i).wait_recv()
            total = total + ybuf[pair, i].astype(jnp.float32)
        for k in range(2):
            half = total[k * rows:(k + 1) * rows, :].astype(jnp.bfloat16)
            @pl.when(is_self(pair, k))
            def _():
                obuf[zh, y // NX] = half
            @pl.when(jnp.logical_not(is_self(pair, k)))
            def _():
                piece[pair, k] = half
                osend(pair, k).start()

    def step_body(n, carry):
        pair, c = n // 3, lax.rem(n, 3)
        @pl.when(jnp.logical_or(jnp.logical_and(odd == 1, pair == 0), jnp.logical_and(odd == 0, n == 2)))
        def _():
            near_step(odd * n)
        @pl.when(pair == 0)
        def _():
            c_step(c)
        @pl.when(jnp.logical_and(odd == 0, jnp.logical_or(n == 2, n == 4)))
        def _():
            near_step(n // 2)
        @pl.when(jnp.logical_and(odd == 0, pair == 0))
        def _():
            arrival(zh, c, 1 - core).wait_recv()
        @pl.when(jnp.logical_and(odd == 0, pair == 3))
        def _():
            for k in range(2):
                arrival(slot(4), c, k).wait_recv()
        @pl.when(jnp.logical_and(odd == 1, pair == 2))
        def _():
            far_step(c)
        left = rbuf[pair_slot(pair), c].reshape(pair_rows, v_ref.shape[2]).astype(jnp.float32)
        for k in range(NX):
            weighted = (left * scale[pl.ds(k, 1), :]).astype(jnp.bfloat16)
            right = cbuf[k, c].reshape(pair_rows, v_ref.shape[2])
            product = lax.dot_general(
                weighted, right, (((1,), (1,)), ((), ())), preferred_element_type=jnp.float32
            )
            @pl.when(c == 0)
            def _():
                acc[k, :, :pair_rows] = product
            @pl.when(c > 0)
            def _():
                acc[k, :, :pair_rows] = acc[k, :, :pair_rows] + product
        @pl.when(c == 2)
        def _():
            finish(pair)
        @pl.when(jnp.logical_and(pair > 0, c == 2))
        def _():
            relay(pair - 1)
        return carry

    for k in range(NX):
        acc[k, :, pair_rows:] = jnp.zeros((pair_rows, acc.shape[2] - pair_rows), jnp.float32)
    lax.fori_loop(0, 12, step_body, 0)
    relay(3)

    got = []
    for h in range(NZ // 2):
        for g in range(2):
            @pl.when(jnp.logical_not(is_local(h, g)))
            def _():
                remote(
                    obuf.at[h, g], obuf.at[h, g], own_sem.at[0, 0], osem.at[h, g],
                    device(x, z, 1 - core, y),
                ).wait_recv()
        got.append(obuf[h, 0].astype(jnp.float32) + obuf[h, 1].astype(jnp.float32))
    for ri in range(2):
        out_ref[ri] = jnp.concatenate(
            [got[h][:, (2 * k + ri) * rows:(2 * k + ri + 1) * rows]
             for h in range(NZ // 2) for k in range(2)],
            axis=1,
        )

    for c in range(3):
        own_copy(0, c).wait_send()
        own_copy(1, c).wait_send()
        for side in range(2):
            for k in range(2):
                near_copy(side, c, k).wait_send()
    @pl.when(odd == 1)
    def _():
        for c in range(3):
            own_copy(2, c).wait_send()
            for side in range(2):
                far_copy(side, c).wait_send()
    for c in range(3):
        cown_copy(0, c).wait_send()
        cown_copy(1, c).wait_send()
        cfwd_copy(c).wait_send()
        for offset in range(NX):
            part_copy(offset, c).wait_send()
    for pair in range(4):
        for i in range(3):
            ysend(pair, i).wait_send()
        for k in range(2):
            @pl.when(jnp.logical_not(is_self(pair, k)))
            def _():
                osend(pair, k).wait_send()


def local(velocity, panel_weight, panel_group, tile_map, group_gain):
    columns, parts, slab = velocity.shape
    half = parts // 2
    blocks = velocity.reshape(columns, 2, half, slab).transpose(2, 1, 0, 3)
    blocks = blocks.reshape(half, 2 * columns, slab)
    block = (half, 2, 2 * columns, slab)
    pair_rows = 4 * columns
    vmem = pl.BlockSpec(memory_space=pltpu.VMEM)
    smem = pl.BlockSpec(memory_space=pltpu.SMEM)
    dma = pltpu.SemaphoreType.DMA
    result = pl.pallas_call(
        kernel,
        out_shape=jax.ShapeDtypeStruct((2, columns, 8 * columns), jnp.float32),
        in_specs=[vmem, vmem, vmem, smem, smem],
        out_specs=vmem,
        scratch_shapes=[
            pltpu.VMEM((NZ // 2,) + block, jnp.bfloat16),
            pltpu.VMEM((NX,) + block, jnp.bfloat16),
            pltpu.VMEM((NX, slab), jnp.float32),
            pltpu.VMEM((NX, pair_rows, pl.cdiv(pair_rows, 128) * 128), jnp.float32),
            pltpu.VMEM((4, 2 * columns, pair_rows), jnp.float32),
            pltpu.VMEM((4, NX, 2 * columns, pair_rows), jnp.bfloat16),
            pltpu.VMEM((4, 3, 2 * columns, pair_rows), jnp.bfloat16),
            pltpu.VMEM((4, 2, columns, pair_rows), jnp.bfloat16),
            pltpu.VMEM((NZ // 2, 2, columns, pair_rows), jnp.bfloat16),
            dma((NZ // 2, 3, 2)),
            dma((NX, 3, 2)),
            dma((4, 3)),
            dma((NZ // 2, 2)),
            dma((3, 3)),
            dma((2, 3, 2)),
            dma((2, 3)),
            dma((2, 3)),
            dma((3,)),
            dma((NX, 3)),
            dma((4, 3)),
            dma((4, 2)),
            dma((2,)),
        ],
        compiler_params=pltpu.CompilerParams(
            collective_id=0, has_side_effects=True, vmem_limit_bytes=40 * 1024 * 1024
        ),
    )(blocks, panel_weight[None, :], panel_group[None, :], tile_map, group_gain)
    return result.transpose(1, 0, 2)


def solution(mesh):
    return jax.shard_map(
        local,
        mesh=mesh,
        in_specs=(P(("row", "col"), None, "panel"), P("panel"), P("panel"), P(), P()),
        out_specs=P(("row", "panel"), None, "col"),
        check_vma=False,
    )
```

```python
import functools

import jax
import jax.numpy as jnp
from jax import lax
from jax.experimental import pallas as pl
from jax.experimental.pallas import tpu as pltpu
from jax.sharding import PartitionSpec as P

MESH = pl.DeviceIdType.MESH
NX = 4
NZ = 8
NY = 8


def device(x, z, core, y):
    return (lax.rem(z, 2) * NX + x, (z // 2) * 2 + core, y)


def kernel(
    v_ref, weight_ref, group_ref, case_ref, gain_ref, out_ref,
    rbuf, cbuf, scale, acc, own, tbuf, ybuf, piece, obuf,
    rsem, csem, ysem, osem, own_sem, near_sem, far_sem, cown_sem, cfwd_sem,
    part_sem, ysend_sem, osend_sem, local_sem,
):
    rows = v_ref.shape[1] // 2
    pair_rows = 4 * rows
    row, col, y = lax.axis_index("row"), lax.axis_index("col"), lax.axis_index("panel")
    zl, x = row // NX, lax.rem(row, NX)
    zh, core = col // 2, lax.rem(col, 2)
    z = 2 * zh + zl
    odd = lax.rem(zl + core, 2)
    tile_row = NX * core + x
    near = 2 - odd

    def chip_z(offset):
        return lax.rem(z + offset + NZ, NZ)

    def chip_x(offset):
        return lax.rem(x + offset + NX, NX)

    def chip_y(offset):
        return lax.rem(y + offset + NY, NY)

    mine = lax.rem(y, NX)
    is_final_self = jnp.logical_and(core == zl, col == NX * zl + mine)

    def is_local(h, g):
        return jnp.logical_and(is_final_self, jnp.logical_and(h == zh, g == y // NX))

    barrier = pltpu.get_barrier_semaphore()

    def greet(target):
        pl.semaphore_signal(barrier, inc=1, device_id=target, device_id_type=MESH)

    for dirn in (1, -1):
        for k in range(2):
            greet(device(x, chip_z(dirn), k, y))
        greet(device(chip_x(dirn), z, core, y))
    greet(device(x, z, 1 - core, y))
    for offset in (1, -1, 2, -2):
        greet((row, col, chip_y(offset)))
    for h in range(NZ // 2):
        for g in range(2):
            source = (NX * (col // NX) + x, 2 * h + zl, NX * g + lax.rem(col, NX))
            @pl.when(jnp.logical_not(is_local(h, g)))
            def _():
                greet(source)
    pl.semaphore_wait(barrier, 19 - jnp.where(is_final_self, 1, 0))

    def remote(src, dst, send, recv, target):
        return pltpu.make_async_remote_copy(
            src_ref=src, dst_ref=dst, send_sem=send, recv_sem=recv,
            device_id=target, device_id_type=MESH,
        )

    def own_copy(target, c):
        where = (chip_z(1), chip_z(-1), z)[target]
        to = zl if target < 2 else 1 - core
        return remote(
            v_ref.at[c], rbuf.at[zh, c, core], own_sem.at[target, c],
            rsem.at[zh, c, core], device(x, where, to, y),
        )

    def cown_copy(target, c):
        to = device(chip_x(1 - 2 * target), z, core, y)
        return remote(
            v_ref.at[c], cbuf.at[x, c, core], cown_sem.at[target, c], csem.at[x, c, core], to
        )

    def part_copy(offset, c):
        k = chip_x(offset)
        src = v_ref.at[c] if offset == 0 else cbuf.at[k, c, core]
        return remote(
            src, cbuf.at[k, c, core], part_sem.at[offset, c], csem.at[k, c, core],
            device(x, z, 1 - core, y),
        )

    local_c = pltpu.make_async_copy(v_ref, cbuf.at[x, :, core], local_sem.at[0])
    local_r = pltpu.make_async_copy(v_ref, rbuf.at[zh, :, core], local_sem.at[1])
    for c in range(3):
        own_copy(0, c).start()
        own_copy(1, c).start()
        if c == 0:
            cown_copy(0, c).start()
            cown_copy(1, c).start()
        part_copy(0, c).start()
        @pl.when(odd == 1)
        def _():
            own_copy(2, c).start()
    local_c.start()
    @pl.when(odd == 0)
    def _():
        local_r.start()

    lanes = lax.broadcasted_iota(jnp.int32, (1, acc.shape[2]), 1)
    imag = jnp.logical_or(
        jnp.logical_and(lanes >= rows, lanes < 2 * rows),
        jnp.logical_and(lanes >= 3 * rows, lanes < 4 * rows),
    )
    for k in range(NX):
        case = case_ref[tile_row, NX * zl + k]
        groups = group_ref[...]
        gain = jnp.zeros(groups.shape, jnp.float32)
        for g in range(gain_ref.shape[0]):
            gain = jnp.where(groups == g, gain_ref[g, case], gain)
        scale[pl.ds(k, 1), :] = weight_ref[...] * gain

    def slot(offset):
        return chip_z(offset) // 2

    def arrival(h, c, k):
        return remote(
            rbuf.at[h, c, k], rbuf.at[h, c, k], own_sem.at[0, 0], rsem.at[h, c, k],
            device(x, chip_z(1), core, y),
        )

    def near_copy(side, c, k):
        dirn = 1 - 2 * side
        h = slot(-dirn * near)
        return remote(
            rbuf.at[h, c, k], rbuf.at[h, c, k], near_sem.at[side, c, k],
            rsem.at[h, c, k], device(x, chip_z(dirn), core, y),
        )

    def far_copy(side, c):
        dirn = 1 - 2 * side
        h = slot(-dirn * 3)
        return remote(
            rbuf.at[h, c, side], rbuf.at[h, c, side], far_sem.at[side, c],
            rsem.at[h, c, side], device(x, chip_z(dirn), core, y),
        )

    def near_step(c):
        for k in range(2):
            for side in range(2):
                arrival(slot((2 * side - 1) * near), c, k).wait_recv()
                near_copy(side, c, k).start()

    def far_step(c):
        for k in range(2):
            for side in range(2):
                arrival(slot((2 * side - 1) * 3), c, k).wait_recv()
                if k == side:
                    far_copy(side, c).start()

    def c_arrival(k, c, which):
        return remote(
            cbuf.at[k, c, which], cbuf.at[k, c, which], own_sem.at[0, 0],
            csem.at[k, c, which], device(x, z, 1 - core, y),
        )

    back = 2 * core - 1

    def cfwd_copy(c):
        k = chip_x(back)
        return remote(
            cbuf.at[k, c, core], cbuf.at[k, c, core], cfwd_sem.at[c],
            csem.at[k, c, core], device(chip_x(-back), z, core, y),
        )

    def c_step(c):
        c_arrival(chip_x(back), c, core).wait_recv()
        cfwd_copy(c).start()
        @pl.when(c < 2)
        def _():
            cown_copy(0, c + 1).start()
            cown_copy(1, c + 1).start()
        c_arrival(chip_x(-back), c, core).wait_recv()
        part_copy(1, c).start()
        part_copy(3, c).start()
        c_arrival(chip_x(2), c, core).wait_recv()
        part_copy(2, c).start()
        for offset in range(NX):
            c_arrival(chip_x(offset), c, 1 - core).wait_recv()

    local_c.wait()
    @pl.when(odd == 0)
    def _():
        local_r.wait()

    def pair_slot(pair):
        even_offset = 2 * (lax.rem(pair + pair // 2, 4) + 2 * (pair // 3))
        odd_offset = (2 * lax.rem(pair, 2) - 1) * (1 + 2 * (pair // 2))
        return slot(jnp.where(odd == 1, odd_offset, even_offset))

    def ysend(pair, i):
        hop = (1, -1, 4 * lax.rem(y, 2) - 2)[i]
        return remote(
            tbuf.at[pair, lax.rem(chip_y(hop), NX)], ybuf.at[pair, i], ysend_sem.at[pair, i],
            ysem.at[pair, i], (row, col, chip_y(hop)),
        )

    def y_arrival(pair, i):
        return remote(
            ybuf.at[pair, i], ybuf.at[pair, i], own_sem.at[0, 0], ysem.at[pair, i],
            (row, col, chip_y(1)),
        )

    lane_cut = ybuf.shape[3]
    left_over = pair_rows - lane_cut
    group = rows // 3

    def pack(halves):
        rest = [
            half[g * group:(g + 1) * group, lane_cut:pair_rows] for half in halves for g in range(3)
        ]
        rest.append(jnp.zeros((group, lane_cut - 6 * left_over), jnp.float32))
        return jnp.concatenate(
            [half[:, :lane_cut] for half in halves] + [jnp.concatenate(rest, axis=1)], axis=0
        )

    def unpack(half):
        rest = jnp.concatenate(
            [half[rows:rows + group, g * left_over:(g + 1) * left_over] for g in range(3)], axis=0
        )
        return jnp.concatenate([half[:rows, :], rest], axis=1)

    def finish(pair):
        for j in range(NX):
            sign = jnp.where(tile_row <= NX * zl + j, 1.0, -1.0).astype(jnp.float32)
            halves = []
            for k in range(2):
                base = k * 2 * rows
                top = acc[j, base:base + rows, :]
                low = acc[j, base + rows:base + 2 * rows, :]
                swapped = jnp.where(
                    imag, pltpu.roll(low, rows, 1), pltpu.roll(low, acc.shape[2] - rows, 1)
                )
                halves.append(jnp.where(imag, swapped - sign * top, top + sign * swapped))
            total = pack(halves)
            @pl.when(mine == j)
            def _():
                own[pair] = total
            @pl.when(mine != j)
            def _():
                tbuf[pair, j] = total.astype(jnp.bfloat16)
        for i in range(3):
            ysend(pair, i).start()

    def osend(pair, k):
        target = (tile_row, NX * zl + mine, 2 * pair_slot(pair) + k)
        there = y // NX
        return remote(
            piece.at[pair, k], obuf.at[zh, there], osend_sem.at[pair, k], osem.at[zh, there], target
        )

    def is_self(pair, k):
        return jnp.logical_and(is_final_self, 2 * pair_slot(pair) + k == y)

    def relay(pair):
        total = own[pair]
        for i in range(3):
            y_arrival(pair, i).wait_recv()
            total = total + ybuf[pair, i].astype(jnp.float32)
        for k in range(2):
            rest = total[2 * rows:2 * rows + group, :]
            if k == 1:
                rest = jnp.concatenate([rest[:, 3 * left_over:], rest[:, :3 * left_over]], axis=1)
            half = jnp.concatenate([total[k * rows:(k + 1) * rows, :], rest], axis=0)
            half = half.astype(jnp.bfloat16)
            @pl.when(is_self(pair, k))
            def _():
                obuf[zh, y // NX] = half
            @pl.when(jnp.logical_not(is_self(pair, k)))
            def _():
                piece[pair, k] = half
                osend(pair, k).start()

    def step_body(n, carry):
        pair, c = n // 3, lax.rem(n, 3)
        @pl.when(jnp.logical_or(jnp.logical_and(odd == 1, pair == 0), jnp.logical_and(odd == 0, n == 2)))
        def _():
            near_step(odd * n)
        @pl.when(pair == 0)
        def _():
            c_step(c)
        @pl.when(jnp.logical_and(odd == 0, jnp.logical_or(n == 2, n == 4)))
        def _():
            near_step(n // 2)
        @pl.when(jnp.logical_and(odd == 0, pair == 0))
        def _():
            arrival(zh, c, 1 - core).wait_recv()
        @pl.when(jnp.logical_and(odd == 0, pair == 3))
        def _():
            for k in range(2):
                arrival(slot(4), c, k).wait_recv()
        @pl.when(jnp.logical_and(odd == 1, pair == 2))
        def _():
            far_step(c)
        left = rbuf[pair_slot(pair), c].reshape(pair_rows, v_ref.shape[2]).astype(jnp.float32)
        for k in range(NX):
            weighted = (left * scale[pl.ds(k, 1), :]).astype(jnp.bfloat16)
            right = cbuf[k, c].reshape(pair_rows, v_ref.shape[2])
            product = lax.dot_general(
                weighted, right, (((1,), (1,)), ((), ())), preferred_element_type=jnp.float32
            )
            @pl.when(c == 0)
            def _():
                acc[k, :, :pair_rows] = product
            @pl.when(c > 0)
            def _():
                acc[k, :, :pair_rows] = acc[k, :, :pair_rows] + product
        @pl.when(c == 2)
        def _():
            finish(pair)
        @pl.when(n >= 10)
        def _():
            relay(n - 10)
        return carry

    for k in range(NX):
        acc[k, :, pair_rows:] = jnp.zeros((pair_rows, acc.shape[2] - pair_rows), jnp.float32)
    lax.fori_loop(0, 12, step_body, 0)
    relay(2)
    relay(3)

    got = []
    for h in range(NZ // 2):
        for g in range(2):
            @pl.when(jnp.logical_not(is_local(h, g)))
            def _():
                remote(
                    obuf.at[h, g], obuf.at[h, g], own_sem.at[0, 0], osem.at[h, g],
                    device(x, z, 1 - core, y),
                ).wait_recv()
        got.append(unpack(obuf[h, 0].astype(jnp.float32) + obuf[h, 1].astype(jnp.float32)))
    for ri in range(2):
        out_ref[ri] = jnp.concatenate(
            [got[h][:, (2 * k + ri) * rows:(2 * k + ri + 1) * rows]
             for h in range(NZ // 2) for k in range(2)],
            axis=1,
        )

    for c in range(3):
        own_copy(0, c).wait_send()
        own_copy(1, c).wait_send()
        for side in range(2):
            for k in range(2):
                near_copy(side, c, k).wait_send()
    @pl.when(odd == 1)
    def _():
        for c in range(3):
            own_copy(2, c).wait_send()
            for side in range(2):
                far_copy(side, c).wait_send()
    for c in range(3):
        cown_copy(0, c).wait_send()
        cown_copy(1, c).wait_send()
        cfwd_copy(c).wait_send()
        for offset in range(NX):
            part_copy(offset, c).wait_send()
    for pair in range(4):
        for i in range(3):
            ysend(pair, i).wait_send()
        for k in range(2):
            @pl.when(jnp.logical_not(is_self(pair, k)))
            def _():
                osend(pair, k).wait_send()


def local(velocity, panel_weight, panel_group, tile_map, group_gain):
    columns, parts, slab = velocity.shape
    half = parts // 2
    blocks = velocity.reshape(columns, 2, half, slab).transpose(2, 1, 0, 3)
    blocks = blocks.reshape(half, 2 * columns, slab)
    block = (half, 2, 2 * columns, slab)
    pair_rows = 4 * columns
    lane_cut = pair_rows // 128 * 128
    packed = (2 * columns + columns // 3, lane_cut)
    packed_half = (columns + columns // 3, lane_cut)
    vmem = pl.BlockSpec(memory_space=pltpu.VMEM)
    smem = pl.BlockSpec(memory_space=pltpu.SMEM)
    dma = pltpu.SemaphoreType.DMA
    result = pl.pallas_call(
        kernel,
        out_shape=jax.ShapeDtypeStruct((2, columns, 8 * columns), jnp.float32),
        in_specs=[vmem, vmem, vmem, smem, smem],
        out_specs=vmem,
        scratch_shapes=[
            pltpu.VMEM((NZ // 2,) + block, jnp.bfloat16),
            pltpu.VMEM((NX,) + block, jnp.bfloat16),
            pltpu.VMEM((NX, slab), jnp.float32),
            pltpu.VMEM((NX, pair_rows, pl.cdiv(pair_rows, 128) * 128), jnp.float32),
            pltpu.VMEM((4,) + packed, jnp.float32),
            pltpu.VMEM((4, NX) + packed, jnp.bfloat16),
            pltpu.VMEM((4, 3) + packed, jnp.bfloat16),
            pltpu.VMEM((4, 2) + packed_half, jnp.bfloat16),
            pltpu.VMEM((NZ // 2, 2) + packed_half, jnp.bfloat16),
            dma((NZ // 2, 3, 2)),
            dma((NX, 3, 2)),
            dma((4, 3)),
            dma((NZ // 2, 2)),
            dma((3, 3)),
            dma((2, 3, 2)),
            dma((2, 3)),
            dma((2, 3)),
            dma((3,)),
            dma((NX, 3)),
            dma((4, 3)),
            dma((4, 2)),
            dma((2,)),
        ],
        compiler_params=pltpu.CompilerParams(
            collective_id=0, has_side_effects=True, vmem_limit_bytes=40 * 1024 * 1024
        ),
    )(blocks, panel_weight[None, :], panel_group[None, :], tile_map, group_gain)
    return result.transpose(1, 0, 2)


def solution(mesh):
    return jax.shard_map(
        local,
        mesh=mesh,
        in_specs=(P(("row", "col"), None, "panel"), P("panel"), P("panel"), P(), P()),
        out_specs=P(("row", "panel"), None, "col"),
        check_vma=False,
    )
```

```python
import functools

import jax
import jax.numpy as jnp
from jax import lax
from jax.experimental import pallas as pl
from jax.experimental.pallas import tpu as pltpu
from jax.sharding import PartitionSpec as P

MESH = pl.DeviceIdType.MESH
NX = 4
NZ = 8
NY = 8


def device(x, z, core, y):
    return (lax.rem(z, 2) * NX + x, (z // 2) * 2 + core, y)


def kernel(
    v_ref, weight_ref, group_ref, case_ref, gain_ref, out_ref,
    rbuf, cbuf, scale, acc, own, tbuf, ybuf, piece, obuf,
    rsem, csem, ysem, osem, own_sem, near_sem, far_sem, cown_sem, cfwd_sem,
    part_sem, ysend_sem, osend_sem, local_sem, inside,
):
    rows = v_ref.shape[1] // 2
    pair_rows = 4 * rows
    row, col, y = lax.axis_index("row"), lax.axis_index("col"), lax.axis_index("panel")
    zl, x = row // NX, lax.rem(row, NX)
    zh, core = col // 2, lax.rem(col, 2)
    z = 2 * zh + zl
    odd = lax.rem(zl + core, 2)
    tile_row = NX * core + x
    near = 2 - odd

    def chip_z(offset):
        return lax.rem(z + offset + NZ, NZ)

    def chip_x(offset):
        return lax.rem(x + offset + NX, NX)

    mine = lax.rem(y, NX)
    is_final_self = jnp.logical_and(core == zl, col == NX * zl + mine)

    def chip_y(offset):
        return lax.rem(y + offset + NY, NY)

    def is_local(h, g):
        return jnp.logical_and(is_final_self, jnp.logical_and(h == zh, g == y // NX))

    barrier = pltpu.get_barrier_semaphore()

    def greet(target):
        pl.semaphore_signal(barrier, inc=1, device_id=target, device_id_type=MESH)

    for dirn in (1, -1):
        for k in range(2):
            greet(device(x, chip_z(dirn), k, y))
        greet(device(chip_x(dirn), z, core, y))
    greet(device(x, z, 1 - core, y))
    for offset in (1, -1, 2, -2):
        greet((row, col, chip_y(offset)))
    pl.semaphore_wait(barrier, 11)

    def tell(n):
        @pl.when(n == 0)
        def _():
            for offset in (2, -2):
                pl.semaphore_signal(
                    inside.at[0], inc=1, device_id=(row, col, chip_y(offset)), device_id_type=MESH
                )
        @pl.when(n > 0)
        def _():
            for dirn in (1, -1):
                for k in range(2):
                    pl.semaphore_signal(
                        inside.at[n], inc=1, device_id=device(x, chip_z(dirn), k, y),
                        device_id_type=MESH,
                    )

    def hear(n):
        pl.semaphore_wait(inside.at[n], jnp.where(n == 0, 2, 4))

    tell(0)

    def remote(src, dst, send, recv, target):
        return pltpu.make_async_remote_copy(
            src_ref=src, dst_ref=dst, send_sem=send, recv_sem=recv,
            device_id=target, device_id_type=MESH,
        )

    def own_copy(target, c):
        where = (chip_z(1), chip_z(-1), z)[target]
        to = zl if target < 2 else 1 - core
        return remote(
            v_ref.at[c], rbuf.at[zh, c, core], own_sem.at[target, c],
            rsem.at[zh, c, core], device(x, where, to, y),
        )

    def cown_copy(target, c):
        to = device(chip_x(1 - 2 * target), z, core, y)
        return remote(
            v_ref.at[c], cbuf.at[x, c, core], cown_sem.at[target, c], csem.at[x, c, core], to
        )

    def part_copy(offset, c):
        k = chip_x(offset)
        src = v_ref.at[c] if offset == 0 else cbuf.at[k, c, core]
        return remote(
            src, cbuf.at[k, c, core], part_sem.at[offset, c], csem.at[k, c, core],
            device(x, z, 1 - core, y),
        )

    local_c = pltpu.make_async_copy(v_ref, cbuf.at[x, :, core], local_sem.at[0])
    local_r = pltpu.make_async_copy(v_ref, rbuf.at[zh, :, core], local_sem.at[1])
    for c in range(3):
        own_copy(0, c).start()
        own_copy(1, c).start()
        if c == 0:
            cown_copy(0, c).start()
            cown_copy(1, c).start()
        part_copy(0, c).start()
        @pl.when(odd == 1)
        def _():
            own_copy(2, c).start()
    local_c.start()
    @pl.when(odd == 0)
    def _():
        local_r.start()

    lanes = lax.broadcasted_iota(jnp.int32, (1, acc.shape[2]), 1)
    imag = jnp.logical_or(
        jnp.logical_and(lanes >= rows, lanes < 2 * rows),
        jnp.logical_and(lanes >= 3 * rows, lanes < 4 * rows),
    )
    for k in range(NX):
        case = case_ref[tile_row, NX * zl + k]
        groups = group_ref[...]
        gain = jnp.zeros(groups.shape, jnp.float32)
        for g in range(gain_ref.shape[0]):
            gain = jnp.where(groups == g, gain_ref[g, case], gain)
        scale[pl.ds(k, 1), :] = weight_ref[...] * gain

    def slot(offset):
        return chip_z(offset) // 2

    def arrival(h, c, k):
        return remote(
            rbuf.at[h, c, k], rbuf.at[h, c, k], own_sem.at[0, 0], rsem.at[h, c, k],
            device(x, chip_z(1), core, y),
        )

    def near_copy(side, c, k):
        dirn = 1 - 2 * side
        h = slot(-dirn * near)
        return remote(
            rbuf.at[h, c, k], rbuf.at[h, c, k], near_sem.at[side, c, k],
            rsem.at[h, c, k], device(x, chip_z(dirn), core, y),
        )

    def far_copy(side, c):
        dirn = 1 - 2 * side
        h = slot(-dirn * 3)
        return remote(
            rbuf.at[h, c, side], rbuf.at[h, c, side], far_sem.at[side, c],
            rsem.at[h, c, side], device(x, chip_z(dirn), core, y),
        )

    def near_step(c):
        for k in range(2):
            for side in range(2):
                arrival(slot((2 * side - 1) * near), c, k).wait_recv()
                near_copy(side, c, k).start()

    def far_step(c):
        for k in range(2):
            for side in range(2):
                arrival(slot((2 * side - 1) * 3), c, k).wait_recv()
                if k == side:
                    far_copy(side, c).start()

    def c_arrival(k, c, which):
        return remote(
            cbuf.at[k, c, which], cbuf.at[k, c, which], own_sem.at[0, 0],
            csem.at[k, c, which], device(x, z, 1 - core, y),
        )

    back = 2 * core - 1

    def cfwd_copy(c):
        k = chip_x(back)
        return remote(
            cbuf.at[k, c, core], cbuf.at[k, c, core], cfwd_sem.at[c],
            csem.at[k, c, core], device(chip_x(-back), z, core, y),
        )

    def c_step(c):
        c_arrival(chip_x(back), c, core).wait_recv()
        cfwd_copy(c).start()
        @pl.when(c < 2)
        def _():
            cown_copy(0, c + 1).start()
            cown_copy(1, c + 1).start()
        c_arrival(chip_x(-back), c, core).wait_recv()
        part_copy(1, c).start()
        part_copy(3, c).start()
        c_arrival(chip_x(2), c, core).wait_recv()
        part_copy(2, c).start()
        for offset in range(NX):
            c_arrival(chip_x(offset), c, 1 - core).wait_recv()

    local_c.wait()
    @pl.when(odd == 0)
    def _():
        local_r.wait()

    def pair_slot(pair):
        even_offset = 2 * (lax.rem(pair + pair // 2, 4) + 2 * (pair // 3))
        odd_offset = (2 * lax.rem(pair, 2) - 1) * (1 + 2 * (pair // 2))
        return slot(jnp.where(odd == 1, odd_offset, even_offset))

    def ysend(pair, i):
        hop = (1, -1, 4 * lax.rem(y, 2) - 2)[i]
        return remote(
            tbuf.at[pair, lax.rem(chip_y(hop), NX)], ybuf.at[pair, i], ysend_sem.at[pair, i],
            ysem.at[pair, i], (row, col, chip_y(hop)),
        )

    def y_arrival(pair, i):
        return remote(
            ybuf.at[pair, i], ybuf.at[pair, i], own_sem.at[0, 0], ysem.at[pair, i],
            (row, col, chip_y(1)),
        )

    lane_cut = ybuf.shape[3]
    left_over = pair_rows - lane_cut
    group = rows // 3

    def pack(halves):
        rest = [
            half[g * group:(g + 1) * group, lane_cut:pair_rows] for half in halves for g in range(3)
        ]
        rest.append(jnp.zeros((group, lane_cut - 6 * left_over), jnp.float32))
        return jnp.concatenate(
            [half[:, :lane_cut] for half in halves] + [jnp.concatenate(rest, axis=1)], axis=0
        )

    def unpack(half):
        rest = jnp.concatenate(
            [half[rows:rows + group, g * left_over:(g + 1) * left_over] for g in range(3)], axis=0
        )
        return jnp.concatenate([half[:rows, :], rest], axis=1)

    def finish(pair):
        for i, offset in enumerate((1, 3, 2, 0)):
            j = lax.rem(mine + offset, NX)
            sign = jnp.where(tile_row <= NX * zl + j, 1.0, -1.0).astype(jnp.float32)
            halves = []
            for k in range(2):
                base = k * 2 * rows
                top = acc[j, base:base + rows, :]
                low = acc[j, base + rows:base + 2 * rows, :]
                swapped = jnp.where(
                    imag, pltpu.roll(low, rows, 1), pltpu.roll(low, acc.shape[2] - rows, 1)
                )
                halves.append(jnp.where(imag, swapped - sign * top, top + sign * swapped))
            if offset:
                tbuf[pair, j] = pack(halves).astype(jnp.bfloat16)
                ysend(pair, i).start()
            else:
                own[pair] = pack(halves)

    def osend(pair, k):
        target = (tile_row, NX * zl + mine, 2 * pair_slot(pair) + k)
        there = y // NX
        return remote(
            piece.at[pair, k], obuf.at[zh, there], osend_sem.at[pair, k], osem.at[zh, there], target
        )

    def is_self(pair, k):
        return jnp.logical_and(is_final_self, 2 * pair_slot(pair) + k == y)

    def relay(pair):
        total = own[pair]
        for i in range(3):
            y_arrival(pair, i).wait_recv()
            total = total + ybuf[pair, i].astype(jnp.float32)
        for k in range(2):
            rest = total[2 * rows:2 * rows + group, :]
            if k == 1:
                rest = jnp.concatenate([rest[:, 3 * left_over:], rest[:, :3 * left_over]], axis=1)
            half = jnp.concatenate([total[k * rows:(k + 1) * rows, :], rest], axis=0)
            half = half.astype(jnp.bfloat16)
            @pl.when(is_self(pair, k))
            def _():
                obuf[zh, y // NX] = half
            @pl.when(jnp.logical_not(is_self(pair, k)))
            def _():
                piece[pair, k] = half
                osend(pair, k).start()

    def step_body(n, carry):
        pair, c = n // 3, lax.rem(n, 3)
        @pl.when(jnp.logical_or(jnp.logical_and(odd == 1, pair == 0), jnp.logical_and(odd == 0, n == 2)))
        def _():
            near_step(odd * n)
        @pl.when(pair == 0)
        def _():
            c_step(c)
        @pl.when(jnp.logical_and(odd == 0, jnp.logical_or(n == 2, n == 4)))
        def _():
            near_step(n // 2)
        @pl.when(jnp.logical_and(odd == 0, pair == 0))
        def _():
            arrival(zh, c, 1 - core).wait_recv()
        @pl.when(jnp.logical_and(odd == 0, pair == 3))
        def _():
            for k in range(2):
                arrival(slot(4), c, k).wait_recv()
        @pl.when(jnp.logical_and(odd == 1, jnp.logical_and(n >= 5, n < 8)))
        def _():
            far_step(n - 5)
        left = rbuf[pair_slot(pair), c].reshape(pair_rows, v_ref.shape[2]).astype(jnp.float32)
        for k in range(NX):
            weighted = (left * scale[pl.ds(k, 1), :]).astype(jnp.bfloat16)
            right = cbuf[k, c].reshape(pair_rows, v_ref.shape[2])
            product = lax.dot_general(
                weighted, right, (((1,), (1,)), ((), ())), preferred_element_type=jnp.float32
            )
            @pl.when(c == 0)
            def _():
                acc[k, :, :pair_rows] = product
            @pl.when(c > 0)
            def _():
                acc[k, :, :pair_rows] = acc[k, :, :pair_rows] + product
        @pl.when(c == 2)
        def _():
            finish(pair)
        @pl.when(jnp.logical_and(lax.rem(n, 2) == 1, n < 11))
        def _():
            hear(n // 2)
            @pl.when(n < 9)
            def _():
                tell(n // 2 + 1)
        @pl.when(n >= 10)
        def _():
            relay(n - 10)
        return carry

    for k in range(NX):
        acc[k, :, pair_rows:] = jnp.zeros((pair_rows, acc.shape[2] - pair_rows), jnp.float32)
    lax.fori_loop(0, 12, step_body, 0)
    relay(2)
    relay(3)

    got = []
    for h in range(NZ // 2):
        for g in range(2):
            @pl.when(jnp.logical_not(is_local(h, g)))
            def _():
                remote(
                    obuf.at[h, g], obuf.at[h, g], own_sem.at[0, 0], osem.at[h, g],
                    device(x, z, 1 - core, y),
                ).wait_recv()
        got.append(unpack(obuf[h, 0].astype(jnp.float32) + obuf[h, 1].astype(jnp.float32)))
    for ri in range(2):
        out_ref[ri] = jnp.concatenate(
            [got[h][:, (2 * k + ri) * rows:(2 * k + ri + 1) * rows]
             for h in range(NZ // 2) for k in range(2)],
            axis=1,
        )

    for c in range(3):
        own_copy(0, c).wait_send()
        own_copy(1, c).wait_send()
        for side in range(2):
            for k in range(2):
                near_copy(side, c, k).wait_send()
    @pl.when(odd == 1)
    def _():
        for c in range(3):
            own_copy(2, c).wait_send()
            for side in range(2):
                far_copy(side, c).wait_send()
    for c in range(3):
        cown_copy(0, c).wait_send()
        cown_copy(1, c).wait_send()
        cfwd_copy(c).wait_send()
        for offset in range(NX):
            part_copy(offset, c).wait_send()
    for pair in range(4):
        for i in range(3):
            ysend(pair, i).wait_send()
        for k in range(2):
            @pl.when(jnp.logical_not(is_self(pair, k)))
            def _():
                osend(pair, k).wait_send()


def local(velocity, panel_weight, panel_group, tile_map, group_gain):
    columns, parts, slab = velocity.shape
    half = parts // 2
    blocks = velocity.reshape(columns, 2, half, slab).transpose(2, 1, 0, 3)
    blocks = blocks.reshape(half, 2 * columns, slab)
    block = (half, 2, 2 * columns, slab)
    pair_rows = 4 * columns
    lane_cut = pair_rows // 128 * 128
    packed = (2 * columns + columns // 3, lane_cut)
    packed_half = (columns + columns // 3, lane_cut)
    vmem = pl.BlockSpec(memory_space=pltpu.VMEM)
    smem = pl.BlockSpec(memory_space=pltpu.SMEM)
    dma = pltpu.SemaphoreType.DMA
    result = pl.pallas_call(
        kernel,
        out_shape=jax.ShapeDtypeStruct((2, columns, 8 * columns), jnp.float32),
        in_specs=[vmem, vmem, vmem, smem, smem],
        out_specs=vmem,
        scratch_shapes=[
            pltpu.VMEM((NZ // 2,) + block, jnp.bfloat16),
            pltpu.VMEM((NX,) + block, jnp.bfloat16),
            pltpu.VMEM((NX, slab), jnp.float32),
            pltpu.VMEM((NX, pair_rows, pl.cdiv(pair_rows, 128) * 128), jnp.float32),
            pltpu.VMEM((4,) + packed, jnp.float32),
            pltpu.VMEM((4, NX) + packed, jnp.bfloat16),
            pltpu.VMEM((4, 3) + packed, jnp.bfloat16),
            pltpu.VMEM((4, 2) + packed_half, jnp.bfloat16),
            pltpu.VMEM((NZ // 2, 2) + packed_half, jnp.bfloat16),
            dma((NZ // 2, 3, 2)),
            dma((NX, 3, 2)),
            dma((4, 3)),
            dma((NZ // 2, 2)),
            dma((3, 3)),
            dma((2, 3, 2)),
            dma((2, 3)),
            dma((2, 3)),
            dma((3,)),
            dma((NX, 3)),
            dma((4, 3)),
            dma((4, 2)),
            dma((2,)),
            pltpu.SemaphoreType.REGULAR((5,)),
        ],
        compiler_params=pltpu.CompilerParams(
            collective_id=0, has_side_effects=True, vmem_limit_bytes=40 * 1024 * 1024
        ),
    )(blocks, panel_weight[None, :], panel_group[None, :], tile_map, group_gain)
    return result.transpose(1, 0, 2)


def solution(mesh):
    return jax.shard_map(
        local,
        mesh=mesh,
        in_specs=(P(("row", "col"), None, "panel"), P("panel"), P("panel"), P(), P()),
        out_specs=P(("row", "panel"), None, "col"),
        check_vma=False,
    )
```

```python
import functools

import jax
import jax.numpy as jnp
from jax import lax
from jax.experimental import pallas as pl
from jax.experimental.pallas import tpu as pltpu
from jax.sharding import PartitionSpec as P

MESH = pl.DeviceIdType.MESH
NX = 4
NZ = 8
NY = 8


def device(x, z, core, y):
    return (lax.rem(z, 2) * NX + x, (z // 2) * 2 + core, y)


def kernel(
    v_ref, weight_ref, group_ref, case_ref, gain_ref, out_ref,
    rbuf, cbuf, scale, acc, own, tbuf, ybuf, piece, obuf,
    rsem, csem, ysem, osem, own_sem, near_sem, far_sem, cown_sem, cfwd_sem,
    part_sem, ysend_sem, osend_sem, local_sem, inside,
):
    rows = v_ref.shape[1] // 2
    pair_rows = 4 * rows
    row, col, y = lax.axis_index("row"), lax.axis_index("col"), lax.axis_index("panel")
    zl, x = row // NX, lax.rem(row, NX)
    zh, core = col // 2, lax.rem(col, 2)
    z = 2 * zh + zl
    odd = lax.rem(zl + core, 2)
    tile_row = NX * core + x
    near = 2 - odd

    def chip_z(offset):
        return lax.rem(z + offset + NZ, NZ)

    def chip_x(offset):
        return lax.rem(x + offset + NX, NX)

    mine = lax.rem(y, NX)
    is_final_self = jnp.logical_and(core == zl, col == NX * zl + mine)

    def chip_y(offset):
        return lax.rem(y + offset + NY, NY)

    def is_local(h, g):
        return jnp.logical_and(is_final_self, jnp.logical_and(h == zh, g == y // NX))

    barrier = pltpu.get_barrier_semaphore()

    def greet(target):
        pl.semaphore_signal(barrier, inc=1, device_id=target, device_id_type=MESH)

    for dirn in (1, -1):
        for k in range(2):
            greet(device(x, chip_z(dirn), k, y))
        greet(device(chip_x(dirn), z, core, y))
    greet(device(x, z, 1 - core, y))
    for offset in (1, -1, 2, -2):
        greet((row, col, chip_y(offset)))
    pl.semaphore_wait(barrier, 11)

    def tell(n):
        @pl.when(n == 0)
        def _():
            for offset in (2, -2):
                pl.semaphore_signal(
                    inside.at[0], inc=1, device_id=(row, col, chip_y(offset)), device_id_type=MESH
                )
        @pl.when(n > 0)
        def _():
            for dirn in (1, -1):
                for k in range(2):
                    pl.semaphore_signal(
                        inside.at[n], inc=1, device_id=device(x, chip_z(dirn), k, y),
                        device_id_type=MESH,
                    )

    def hear(n):
        pl.semaphore_wait(inside.at[n], jnp.where(n == 0, 2, 4))

    tell(0)

    def remote(src, dst, send, recv, target):
        return pltpu.make_async_remote_copy(
            src_ref=src, dst_ref=dst, send_sem=send, recv_sem=recv,
            device_id=target, device_id_type=MESH,
        )

    def own_copy(target, c):
        where = (chip_z(1), chip_z(-1), z)[target]
        to = zl if target < 2 else 1 - core
        return remote(
            v_ref.at[c], rbuf.at[zh, c, core], own_sem.at[target, c],
            rsem.at[zh, c, core], device(x, where, to, y),
        )

    def cown_copy(target, c):
        to = device(chip_x(1 - 2 * target), z, core, y)
        return remote(
            v_ref.at[c], cbuf.at[x, c, core], cown_sem.at[target, c], csem.at[x, c, core], to
        )

    def part_copy(offset, c):
        k = chip_x(offset)
        src = v_ref.at[c] if offset == 0 else cbuf.at[k, c, core]
        return remote(
            src, cbuf.at[k, c, core], part_sem.at[offset, c], csem.at[k, c, core],
            device(x, z, 1 - core, y),
        )

    local_c = pltpu.make_async_copy(v_ref, cbuf.at[x, :, core], local_sem.at[0])
    local_r = pltpu.make_async_copy(v_ref, rbuf.at[zh, :, core], local_sem.at[1])
    for c in range(3):
        if c == 0:
            cown_copy(0, c).start()
            cown_copy(1, c).start()
        part_copy(0, c).start()
        own_copy(0, c).start()
        own_copy(1, c).start()
        @pl.when(odd == 1)
        def _():
            own_copy(2, c).start()
    local_c.start()
    @pl.when(odd == 0)
    def _():
        local_r.start()

    lanes = lax.broadcasted_iota(jnp.int32, (1, acc.shape[2]), 1)
    imag = jnp.logical_or(
        jnp.logical_and(lanes >= rows, lanes < 2 * rows),
        jnp.logical_and(lanes >= 3 * rows, lanes < 4 * rows),
    )
    for k in range(NX):
        case = case_ref[tile_row, NX * zl + k]
        groups = group_ref[...]
        gain = jnp.zeros(groups.shape, jnp.float32)
        for g in range(gain_ref.shape[0]):
            gain = jnp.where(groups == g, gain_ref[g, case], gain)
        scale[pl.ds(k, 1), :] = weight_ref[...] * gain

    def slot(offset):
        return chip_z(offset) // 2

    def arrival(h, c, k):
        return remote(
            rbuf.at[h, c, k], rbuf.at[h, c, k], own_sem.at[0, 0], rsem.at[h, c, k],
            device(x, chip_z(1), core, y),
        )

    def near_copy(side, c, k):
        dirn = 1 - 2 * side
        h = slot(-dirn * near)
        return remote(
            rbuf.at[h, c, k], rbuf.at[h, c, k], near_sem.at[side, c, k],
            rsem.at[h, c, k], device(x, chip_z(dirn), core, y),
        )

    def far_copy(side, c):
        dirn = 1 - 2 * side
        h = slot(-dirn * 3)
        return remote(
            rbuf.at[h, c, side], rbuf.at[h, c, side], far_sem.at[side, c],
            rsem.at[h, c, side], device(x, chip_z(dirn), core, y),
        )

    def near_step(c):
        for k in range(2):
            for side in range(2):
                arrival(slot((2 * side - 1) * near), c, k).wait_recv()
                near_copy(side, c, k).start()

    def far_step(c):
        for k in range(2):
            for side in range(2):
                arrival(slot((2 * side - 1) * 3), c, k).wait_recv()
                if k == side:
                    far_copy(side, c).start()

    def c_arrival(k, c, which):
        return remote(
            cbuf.at[k, c, which], cbuf.at[k, c, which], own_sem.at[0, 0],
            csem.at[k, c, which], device(x, z, 1 - core, y),
        )

    back = 2 * core - 1

    def cfwd_copy(c):
        k = chip_x(back)
        return remote(
            cbuf.at[k, c, core], cbuf.at[k, c, core], cfwd_sem.at[c],
            csem.at[k, c, core], device(chip_x(-back), z, core, y),
        )

    def c_step(c):
        c_arrival(chip_x(back), c, core).wait_recv()
        cfwd_copy(c).start()
        @pl.when(c < 2)
        def _():
            cown_copy(0, c + 1).start()
            cown_copy(1, c + 1).start()
        c_arrival(chip_x(-back), c, core).wait_recv()
        part_copy(1, c).start()
        part_copy(3, c).start()
        c_arrival(chip_x(2), c, core).wait_recv()
        part_copy(2, c).start()
        for offset in range(NX):
            c_arrival(chip_x(offset), c, 1 - core).wait_recv()

    local_c.wait()
    @pl.when(odd == 0)
    def _():
        local_r.wait()

    def pair_slot(pair):
        even_offset = 2 * (lax.rem(pair + pair // 2, 4) + 2 * (pair // 3))
        odd_offset = (2 * lax.rem(pair, 2) - 1) * (1 + 2 * (pair // 2))
        return slot(jnp.where(odd == 1, odd_offset, even_offset))

    def ysend(pair, i):
        hop = (1, -1, 4 * lax.rem(y, 2) - 2)[i]
        return remote(
            tbuf.at[pair, lax.rem(chip_y(hop), NX)], ybuf.at[pair, i], ysend_sem.at[pair, i],
            ysem.at[pair, i], (row, col, chip_y(hop)),
        )

    def y_arrival(pair, i):
        return remote(
            ybuf.at[pair, i], ybuf.at[pair, i], own_sem.at[0, 0], ysem.at[pair, i],
            (row, col, chip_y(1)),
        )

    lane_cut = ybuf.shape[3]
    left_over = pair_rows - lane_cut
    group = rows // 3

    def pack(halves):
        rest = [
            half[g * group:(g + 1) * group, lane_cut:pair_rows] for half in halves for g in range(3)
        ]
        rest.append(jnp.zeros((group, lane_cut - 6 * left_over), jnp.float32))
        return jnp.concatenate(
            [half[:, :lane_cut] for half in halves] + [jnp.concatenate(rest, axis=1)], axis=0
        )

    def unpack(half):
        rest = jnp.concatenate(
            [half[rows:rows + group, g * left_over:(g + 1) * left_over] for g in range(3)], axis=0
        )
        return jnp.concatenate([half[:rows, :], rest], axis=1)

    def finish(pair):
        for i, offset in enumerate((1, 3, 2, 0)):
            j = lax.rem(mine + offset, NX)
            sign = jnp.where(tile_row <= NX * zl + j, 1.0, -1.0).astype(jnp.float32)
            halves = []
            for k in range(2):
                base = k * 2 * rows
                top = acc[j, base:base + rows, :]
                low = acc[j, base + rows:base + 2 * rows, :]
                swapped = jnp.where(
                    imag, pltpu.roll(low, rows, 1), pltpu.roll(low, acc.shape[2] - rows, 1)
                )
                halves.append(jnp.where(imag, swapped - sign * top, top + sign * swapped))
            if offset:
                tbuf[pair, j] = pack(halves).astype(jnp.bfloat16)
                ysend(pair, i).start()
            else:
                own[pair] = pack(halves)

    def osend(pair, k):
        target = (tile_row, NX * zl + mine, 2 * pair_slot(pair) + k)
        there = y // NX
        return remote(
            piece.at[pair, k], obuf.at[zh, there], osend_sem.at[pair, k], osem.at[zh, there], target
        )

    def is_self(pair, k):
        return jnp.logical_and(is_final_self, 2 * pair_slot(pair) + k == y)

    def relay(pair):
        total = own[pair]
        for i in range(3):
            y_arrival(pair, i).wait_recv()
            total = total + ybuf[pair, i].astype(jnp.float32)
        for k in range(2):
            rest = total[2 * rows:2 * rows + group, :]
            if k == 1:
                rest = jnp.concatenate([rest[:, 3 * left_over:], rest[:, :3 * left_over]], axis=1)
            half = jnp.concatenate([total[k * rows:(k + 1) * rows, :], rest], axis=0)
            half = half.astype(jnp.bfloat16)
            @pl.when(is_self(pair, k))
            def _():
                obuf[zh, y // NX] = half
            @pl.when(jnp.logical_not(is_self(pair, k)))
            def _():
                piece[pair, k] = half
                osend(pair, k).start()

    def step_body(n, carry):
        pair, c = n // 3, lax.rem(n, 3)
        @pl.when(jnp.logical_or(jnp.logical_and(odd == 1, pair == 0), jnp.logical_and(odd == 0, n == 2)))
        def _():
            near_step(odd * n)
        @pl.when(pair == 0)
        def _():
            c_step(c)
        @pl.when(jnp.logical_and(odd == 0, jnp.logical_or(n == 2, n == 4)))
        def _():
            near_step(n // 2)
        @pl.when(jnp.logical_and(odd == 0, pair == 0))
        def _():
            arrival(zh, c, 1 - core).wait_recv()
        @pl.when(jnp.logical_and(odd == 0, pair == 3))
        def _():
            for k in range(2):
                arrival(slot(4), c, k).wait_recv()
        @pl.when(jnp.logical_and(odd == 1, jnp.logical_and(n >= 5, n < 8)))
        def _():
            far_step(n - 5)
        left = rbuf[pair_slot(pair), c].reshape(pair_rows, v_ref.shape[2]).astype(jnp.float32)
        for k in range(NX):
            weighted = (left * scale[pl.ds(k, 1), :]).astype(jnp.bfloat16)
            right = cbuf[k, c].reshape(pair_rows, v_ref.shape[2])
            product = lax.dot_general(
                weighted, right, (((1,), (1,)), ((), ())), preferred_element_type=jnp.float32
            )
            @pl.when(c == 0)
            def _():
                acc[k, :, :pair_rows] = product
            @pl.when(c > 0)
            def _():
                acc[k, :, :pair_rows] = acc[k, :, :pair_rows] + product
        @pl.when(c == 2)
        def _():
            finish(pair)
        @pl.when(jnp.logical_and(lax.rem(n, 2) == 1, n < 11))
        def _():
            hear(n // 2)
            @pl.when(n < 9)
            def _():
                tell(n // 2 + 1)
        @pl.when(n >= 10)
        def _():
            relay(n - 10)
        return carry

    for k in range(NX):
        acc[k, :, pair_rows:] = jnp.zeros((pair_rows, acc.shape[2] - pair_rows), jnp.float32)
    lax.fori_loop(0, 12, step_body, 0)
    relay(2)
    relay(3)

    got = []
    for h in range(NZ // 2):
        for g in range(2):
            @pl.when(jnp.logical_not(is_local(h, g)))
            def _():
                remote(
                    obuf.at[h, g], obuf.at[h, g], own_sem.at[0, 0], osem.at[h, g],
                    device(x, z, 1 - core, y),
                ).wait_recv()
        got.append(unpack(obuf[h, 0].astype(jnp.float32) + obuf[h, 1].astype(jnp.float32)))
    for ri in range(2):
        out_ref[ri] = jnp.concatenate(
            [got[h][:, (2 * k + ri) * rows:(2 * k + ri + 1) * rows]
             for h in range(NZ // 2) for k in range(2)],
            axis=1,
        )

    for c in range(3):
        own_copy(0, c).wait_send()
        own_copy(1, c).wait_send()
        for side in range(2):
            for k in range(2):
                near_copy(side, c, k).wait_send()
    @pl.when(odd == 1)
    def _():
        for c in range(3):
            own_copy(2, c).wait_send()
            for side in range(2):
                far_copy(side, c).wait_send()
    for c in range(3):
        cown_copy(0, c).wait_send()
        cown_copy(1, c).wait_send()
        cfwd_copy(c).wait_send()
        for offset in range(NX):
            part_copy(offset, c).wait_send()
    for pair in range(4):
        for i in range(3):
            ysend(pair, i).wait_send()
        for k in range(2):
            @pl.when(jnp.logical_not(is_self(pair, k)))
            def _():
                osend(pair, k).wait_send()


def local(velocity, panel_weight, panel_group, tile_map, group_gain):
    columns, parts, slab = velocity.shape
    half = parts // 2
    blocks = velocity.reshape(columns, 2, half, slab).transpose(2, 1, 0, 3)
    blocks = blocks.reshape(half, 2 * columns, slab)
    block = (half, 2, 2 * columns, slab)
    pair_rows = 4 * columns
    lane_cut = pair_rows // 128 * 128
    packed = (2 * columns + columns // 3, lane_cut)
    packed_half = (columns + columns // 3, lane_cut)
    vmem = pl.BlockSpec(memory_space=pltpu.VMEM)
    smem = pl.BlockSpec(memory_space=pltpu.SMEM)
    dma = pltpu.SemaphoreType.DMA
    result = pl.pallas_call(
        kernel,
        out_shape=jax.ShapeDtypeStruct((2, columns, 8 * columns), jnp.float32),
        in_specs=[vmem, vmem, vmem, smem, smem],
        out_specs=vmem,
        scratch_shapes=[
            pltpu.VMEM((NZ // 2,) + block, jnp.bfloat16),
            pltpu.VMEM((NX,) + block, jnp.bfloat16),
            pltpu.VMEM((NX, slab), jnp.float32),
            pltpu.VMEM((NX, pair_rows, pl.cdiv(pair_rows, 128) * 128), jnp.float32),
            pltpu.VMEM((4,) + packed, jnp.float32),
            pltpu.VMEM((4, NX) + packed, jnp.bfloat16),
            pltpu.VMEM((4, 3) + packed, jnp.bfloat16),
            pltpu.VMEM((4, 2) + packed_half, jnp.bfloat16),
            pltpu.VMEM((NZ // 2, 2) + packed_half, jnp.bfloat16),
            dma((NZ // 2, 3, 2)),
            dma((NX, 3, 2)),
            dma((4, 3)),
            dma((NZ // 2, 2)),
            dma((3, 3)),
            dma((2, 3, 2)),
            dma((2, 3)),
            dma((2, 3)),
            dma((3,)),
            dma((NX, 3)),
            dma((4, 3)),
            dma((4, 2)),
            dma((2,)),
            pltpu.SemaphoreType.REGULAR((5,)),
        ],
        compiler_params=pltpu.CompilerParams(
            collective_id=0, has_side_effects=True, vmem_limit_bytes=40 * 1024 * 1024
        ),
    )(blocks, panel_weight[None, :], panel_group[None, :], tile_map, group_gain)
    return result.transpose(1, 0, 2)


def solution(mesh):
    return jax.shard_map(
        local,
        mesh=mesh,
        in_specs=(P(("row", "col"), None, "panel"), P("panel"), P("panel"), P(), P()),
        out_specs=P(("row", "panel"), None, "col"),
        check_vma=False,
    )
```
